256 devices in a mesh: row: 8 (over y, core), col: 16 (over z, x_hi), layer: 2 (over x_lo).
Axes of the slice: x: 4 (x_hi: 2, x_lo: 2; x = x_hi * 2 + x_lo), y: 4, z: 8, core: 2. Of those that a mesh axis runs over, the one named last changes fastest.
Arguments:
- a_tiles: float32 [128, 2, 7, 128, 128], P(('row', 'col'), 'layer'), may hold values from -0.5 to 0.5
- a_cols: int32 [128, 2, 7], P(('row', 'col'), 'layer'), may hold values from -1 to 255, as said below
- b_tiles: float32 [256, 2, 7, 128, 128], P(('row', 'col'), 'layer'), may hold values from -6 to 6
- b_rows: int32 [256, 2, 7], P(('row', 'col'), 'layer'), may hold values from 0 to 255, as said below
- c_cols: int32 [128, 16, 4], P('row', 'col'), may hold values from 0 to 255, as said below
Outputs:
- c_tiles: float32 [128, 16, 4, 128, 128], P('row', 'col', 'layer')
The draws below stay inside these ranges and needn't reach their ends.
Inputs may be any that keep to these rules, and one draw needn't show every extreme that they name: In a_cols[i, h, :] the used slots come first and hold distinct block columns in [h * 128, (h + 1) * 128); the unused ones hold -1. Some block rows use all 7 slots in each half, others few. b_rows[j, h, :] holds 7 distinct block rows in [h * 128, (h + 1) * 128). c_cols[i, g, :] holds 4 distinct block columns j with (j // 2) % 16 == g.
All inputs are finite; a program needn't handle non-finite values.
Results may differ from the reference program's by a relative error of at most 0.0003.
Values sent between devices are 32-bit elements; how exact they have to be, the bound alone decides.
A program may use at most 128 MiB of HBM per device.

```python
import jax
import jax.numpy as jnp
from jax import lax

TILE = 128
NBLK = 256
RAH = 7
RBH = 7
RCC = 4
MROWS = 128
N_ROW = 8
N_COL = 16
N_LAYER = 2


def row_clusters(key):
    return jax.random.randint(jax.random.fold_in(key, 91), (MROWS,), 0, 4).astype(jnp.int32)


def draw_a_cols(key, part):
    half_count = NBLK // N_LAYER
    quarter = half_count // 4
    window = min(quarter, 2 * max(RAH, RBH))
    clusters = row_clusters(key)

    def one_slot(index):
        sub_key = jax.random.fold_in(key, index)
        layer_id = index % N_LAYER
        row_id = index // N_LAYER
        start = clusters[row_id] * quarter + layer_id * half_count
        picks = jax.random.permutation(sub_key, window)[:RAH].astype(jnp.int32) + start
        heavy = (jax.random.randint(jax.random.fold_in(sub_key, 7), (), 0, 4) == 0) | (row_id == 0)
        light = jax.random.randint(jax.random.fold_in(sub_key, 11), (), 1, RAH // 2 + 1)
        live = jnp.where(heavy, RAH, light)
        slots = jnp.arange(RAH, dtype=jnp.int32)
        return jnp.where(slots < live, picks, -1).astype(jnp.int32)
    values = jax.vmap(one_slot)(jnp.arange(MROWS * N_LAYER, dtype=jnp.int32))
    return values.reshape(MROWS, N_LAYER, RAH)


def draw_b_rows(key, part):
    half_count = NBLK // N_LAYER
    quarter = half_count // 4
    window = min(quarter, 2 * max(RAH, RBH))
    block_width = NBLK // (N_ROW * N_COL)

    def one_slot(index):
        sub_key = jax.random.fold_in(key, index + 3)
        column = index // N_LAYER
        layer_id = index % N_LAYER
        local = column // block_width // N_COL * block_width + column % block_width
        start = local % 4 * quarter + layer_id * half_count
        picks = jax.random.permutation(sub_key, window)[:RBH].astype(jnp.int32)
        return picks + start
    values = jax.vmap(one_slot)(jnp.arange(NBLK * N_LAYER, dtype=jnp.int32))
    return values.reshape(NBLK, N_LAYER, RBH).astype(jnp.int32)


def draw_c_cols(key, part):
    block_width = NBLK // (N_ROW * N_COL)
    per_cluster = NBLK // N_COL // 4
    clusters = row_clusters(key)

    def one_slot(index):
        sub_key = jax.random.fold_in(key, index + 5)
        row_id = index // N_COL
        group = index % N_COL
        local = jax.random.permutation(sub_key, per_cluster)[:RCC].astype(jnp.int32) * 4 + clusters[row_id]
        return (local // block_width * N_COL + group) * block_width + local % block_width
    values = jax.vmap(one_slot)(jnp.arange(MROWS * N_COL, dtype=jnp.int32))
    return values.reshape(MROWS, N_COL, RCC).astype(jnp.int32)


def block_scale(rng, shape, shards, smallest, high):
    factor_of, own = 1.0, jax.random.fold_in(rng, 6)
    for dim, shards_of in shards:
        heights = jnp.exp(jax.random.uniform(jax.random.fold_in(own, dim), (shards_of,), jnp.float32, smallest / len(shards), high / len(shards)))
        factor_of = factor_of * jnp.repeat(heights, shape[dim] // shards_of).reshape([-1 if axis == dim else 1 for axis in range(len(shape))])
    return factor_of


def bell_draw(stream_key, extent, scale, limit, pieces=(), kind=jnp.bfloat16):
    result = scale * jax.random.normal(stream_key, extent, jnp.float32)
    if pieces:
        result = result * block_scale(stream_key, extent, pieces, -0.22, 0.18)
    return jnp.clip(result, -limit, limit).astype(kind)


def setup_inputs(seed: int = 0) -> dict:
    splits = jax.random.split(jax.random.key(seed), 6)
    a_tiles = bell_draw(splits[0], (MROWS, N_LAYER, RAH, TILE, TILE), TILE ** -0.5, 0.5, ((0, 128), (1, 2)), jnp.float32)
    a_cols = draw_a_cols(jax.random.fold_in(splits[5], 71), 0)
    b_tiles = bell_draw(splits[2], (NBLK, N_LAYER, RBH, TILE, TILE), 1.0, 6.0, ((0, 128), (1, 2)), jnp.float32)
    b_rows = draw_b_rows(jax.random.fold_in(splits[5], 71), 0)
    c_cols = draw_c_cols(jax.random.fold_in(splits[5], 71), 0)
    return dict(a_tiles=a_tiles, a_cols=a_cols, b_tiles=b_tiles, b_rows=b_rows, c_cols=c_cols)


def reference(a_tiles, a_cols, b_tiles, b_rows, c_cols):
    halves = b_rows.shape[1]
    slot_count = b_rows.shape[2]
    b_flat = b_tiles.reshape((-1,) + b_tiles.shape[3:])

    def one_row(inputs):
        a_row, a_index, wanted = inputs
        columns = wanted.reshape(-1).astype(jnp.int32)
        col_rows = b_rows[columns]
        matches = (col_rows[:, :, None, :] == a_index[None, :, :, None]) & (a_index >= 0)[None, :, :, None]
        present = jnp.any(matches, axis=3)
        position = jnp.argmax(matches, axis=3).astype(jnp.int32)
        layer_ids = jnp.arange(halves, dtype=jnp.int32)
        flat_index = (columns[:, None, None] * halves + layer_ids[None, :, None]) * slot_count + position
        chosen = jnp.take(b_flat, flat_index.reshape(-1), axis=0)
        chosen = chosen.reshape(flat_index.shape + b_flat.shape[1:])
        chosen = jnp.where(present[..., None, None], chosen, jnp.zeros((), chosen.dtype))
        product = jnp.einsum("heab,qhebc->qac", a_row, chosen, precision=lax.Precision.HIGHEST)
        return product.reshape(wanted.shape + product.shape[1:])

    return lax.map(one_row, (a_tiles, a_cols, c_cols))
```

```python
import jax
import jax.numpy as jnp
from jax import lax
from jax.experimental import pallas as pl
from jax.experimental.pallas import tpu as pltpu
from jax.sharding import PartitionSpec as P

MESH = pl.DeviceIdType.MESH
TILE = 128
SLOTS = 7
A_ROWS = SLOTS * TILE
B_TILES = 2 * SLOTS
B_ROWS = B_TILES * TILE
N_ROW, N_COL = 8, 16
B_ALL = N_ROW * B_TILES
HALF_A = A_ROWS // 2
HALF_B = B_ROWS // 2


def source_col(k, z, x_hi):
    distance = (k + 2) // 4
    other = (k // 2 + 1 + (15 - k) // 15 + k // 15) % 2
    sign = 2 * (k % 2) - 1
    return ((z + sign * distance + 8) % 8) * 2 + (x_hi + other) % 2


def kernel(
    want_ref,
    a_index_ref,
    b_index_ref,
    a_ref,
    b_ref,
    out_ref,
    a_all,
    b_all,
    b_hi,
    b_lo,
    a_index_all,
    b_index_all,
    table_vmem,
    table,
    lhs,
    rhs,
    to_send,
    own_part,
    arrived,
    local_sem,
    ai_send,
    ai_recv,
    bi_send,
    bi_recv,
    a_send,
    a_recv,
    b_send,
    b_recv,
    c_send,
    c_recv,
    out_sem,
):
    row, col, layer = lax.axis_index("row"), lax.axis_index("col"), lax.axis_index("layer")
    z, x_hi = col // 2, col % 2
    y, core = row // 2, row % 2

    def at(r, c, l):
        return (r, c, l)

    z_up = at(row, (col + 2) % N_COL, layer)
    z_down = at(row, (col + N_COL - 2) % N_COL, layer)
    x_far = at(row, z * 2 + (x_hi + 1) % 2, layer)
    y_up_row, y_down_row, y_far_row = (row + 2) % N_ROW, (row + 6) % N_ROW, (row + 4) % N_ROW
    y_up, y_down = at(y_up_row, col, layer), at(y_down_row, col, layer)
    sibling_row = y * 2 + (core + 1) % 2
    sibling = at(sibling_row, col, layer)
    sib_up, sib_down, sib_far = (
        (sibling_row + 2) % N_ROW,
        (sibling_row + 6) % N_ROW,
        (sibling_row + 4) % N_ROW,
    )
    partner = at(row, col, 1 - layer)

    def remote(src, dst, send_sem, recv_sem, device):
        return pltpu.make_async_remote_copy(
            src_ref=src,
            dst_ref=dst,
            send_sem=send_sem,
            recv_sem=recv_sem,
            device_id=device,
            device_id_type=MESH,
        )

    barrier = pltpu.get_barrier_semaphore()

    @pl.loop(1, N_COL)
    def _(d):
        pl.semaphore_signal(
            barrier, inc=1, device_id=at(row, (col + d) % N_COL, layer), device_id_type=MESH
        )

    @pl.loop(1, N_ROW)
    def _(d):
        pl.semaphore_signal(
            barrier, inc=1, device_id=at((row + d) % N_ROW, col, layer), device_id_type=MESH
        )

    pl.semaphore_signal(barrier, inc=1, device_id=partner, device_id_type=MESH)
    pl.semaphore_wait(barrier, N_COL + N_ROW - 1)

    def a_index_copy(d):
        return remote(
            a_index_ref,
            a_index_all.at[col],
            ai_send.at[d],
            ai_recv.at[d],
            at(row, (col + d) % N_COL, layer),
        )

    def b_index_copy(d):
        return remote(
            b_index_ref,
            b_index_all.at[row],
            bi_send.at[d],
            bi_recv.at[d],
            at((row + d) % N_ROW, col, layer),
        )

    @pl.loop(1, N_ROW)
    def _(d):
        b_index_copy(d).start()

    @pl.loop(1, N_COL)
    def _(d):
        a_index_copy(d).start()

    first, second = pl.ds(0, HALF_B), pl.ds(HALF_B, HALF_B)
    b_own_up = remote(b_ref, b_all.at[row], b_send.at[0], b_recv.at[0], y_up)
    b_own_down = remote(b_ref, b_all.at[row], b_send.at[1], b_recv.at[1], y_down)
    b_own_sib = remote(b_ref, b_all.at[row], b_send.at[2], b_recv.at[4], sibling)
    b_fwd_up = remote(
        b_all.at[y_down_row, first], b_all.at[y_down_row, first], b_send.at[3], b_recv.at[2], y_up
    )
    b_fwd_down = remote(
        b_all.at[y_up_row, second], b_all.at[y_up_row, second], b_send.at[4], b_recv.at[3], y_down
    )
    b_down_sib = remote(
        b_all.at[y_down_row], b_all.at[y_down_row], b_send.at[5], b_recv.at[5], sibling
    )
    b_up_sib = remote(b_all.at[y_up_row], b_all.at[y_up_row], b_send.at[6], b_recv.at[6], sibling)
    b_far_sib = [
        remote(
            b_all.at[y_far_row, part],
            b_all.at[y_far_row, part],
            b_send.at[7 + n],
            b_recv.at[7 + n],
            sibling,
        )
        for n, part in enumerate((first, second))
    ]
    b_own_up.start()
    b_own_down.start()

    a_far = remote(a_ref, a_all.at[1], a_send.at[16], a_recv.at[1], x_far)
    a_up = remote(a_ref, a_all.at[2], a_send.at[14], a_recv.at[2], z_up)
    a_down = remote(a_ref, a_all.at[3], a_send.at[15], a_recv.at[3], z_down)
    a_far.start()
    a_up.start()
    a_down.start()
    b_own_sib.start()
    a_local = pltpu.make_async_copy(a_ref, a_all.at[0], local_sem.at[0])
    b_local = pltpu.make_async_copy(b_ref, b_all.at[row], local_sem.at[1])
    a_local.start()
    b_local.start()

    a_index_all[col] = a_index_ref[...]
    b_index_all[row] = b_index_ref[...]
    b_hi[B_ALL] = jnp.zeros((TILE, TILE), jnp.bfloat16)
    b_lo[B_ALL] = jnp.zeros((TILE, TILE), jnp.bfloat16)

    @pl.loop(1, N_ROW)
    def _(d):
        b_index_copy(d).wait()

    @pl.loop(1, N_COL)
    def _(d):
        a_index_copy(d).wait()

    b_index = b_index_all[0]
    for r in range(1, N_ROW):
        b_index = jnp.maximum(b_index, b_index_all[r])
    lane = lax.broadcasted_iota(jnp.int32, (8, TILE), 1)
    panel = lane // SLOTS

    def one_row(i, found):
        a_index = a_index_all[i]
        for q in range(4):
            wanted = want_ref[i, q]
            wanted_panel = wanted // 32 * 2 + wanted % 2
            match = (a_index == b_index) & (panel == wanted_panel)
            position = jnp.min(jnp.where(match, lane, B_ALL), axis=1, keepdims=True)
            found = jnp.where(lane == i * 4 + q, position, found)
        return found

    table_vmem[...] = lax.fori_loop(0, N_COL, one_row, jnp.full((8, TILE), B_ALL, jnp.int32))
    to_table = pltpu.make_async_copy(table_vmem, table, local_sem.at[2])
    to_table.start()
    to_table.wait()

    def split_b(r):
        @pl.loop(0, B_TILES)
        def _(t):
            value = b_all[r, pl.ds(pl.multiple_of(t * TILE, TILE), TILE), :]
            hi = value.astype(jnp.bfloat16)
            b_hi[r * B_TILES + t] = hi
            b_lo[r * B_TILES + t] = (value - hi.astype(jnp.float32)).astype(jnp.bfloat16)

    def a_forward(k):
        ahead = (col + (1 - k % 2) * 2 + (k % 2) * (N_COL - 2)) % N_COL
        return remote(
            a_all.at[k], a_all.at[k + 4], a_send.at[k], a_recv.at[k + 4], at(row, ahead, layer)
        )

    def a_forward_half(k):
        ahead = (col + (1 - k % 2) * 2 + (k % 2) * (N_COL - 2)) % N_COL
        part = pl.ds(pl.multiple_of((k % 2) * HALF_A, HALF_A), HALF_A)
        return remote(
            a_all.at[k, part],
            a_all.at[14 + (k - 10) // 2, part],
            a_send.at[k],
            a_recv.at[k + 4],
            at(row, ahead, layer),
        )

    a_far_up = remote(a_all.at[1], a_all.at[4], a_send.at[0], a_recv.at[4], z_up)
    a_far_down = remote(a_all.at[1], a_all.at[5], a_send.at[1], a_recv.at[5], z_down)

    def a_arrival(k):
        return remote(a_all.at[k], a_all.at[k], a_send.at[k], a_recv.at[k], z_up)

    def a_arrival_half(k, n):
        part = pl.ds(n * HALF_A, HALF_A)
        return remote(
            a_all.at[k, part],
            a_all.at[k, part],
            a_send.at[k],
            a_recv.at[14 + 2 * (k - 14) + n],
            z_up,
        )

    b_local.wait()
    split_b(row)
    for k in (2, 3):
        a_arrival(k).wait_recv()
        a_forward(k).start()
    b_own_sib.wait_recv()
    split_b(sibling_row)
    a_arrival(1).wait_recv()
    a_far_up.start()
    a_far_down.start()
    b_own_up.wait_recv()
    b_fwd_up.start()
    b_down_sib.start()
    b_own_down.wait_recv()
    b_fwd_down.start()
    b_up_sib.start()
    split_b(y_down_row)
    split_b(y_up_row)
    b_down_sib.wait_recv()
    split_b(sib_down)
    b_up_sib.wait_recv()
    split_b(sib_up)
    for k in (6, 7):
        a_arrival(k).wait_recv()
        a_forward(k).start()
    b_fwd_up.wait_recv()
    b_far_sib[0].start()
    b_fwd_down.wait_recv()
    b_far_sib[1].start()
    split_b(y_far_row)
    for k in (4, 5):
        a_arrival(k).wait_recv()
        a_forward(k).start()
    b_far_sib[0].wait_recv()
    b_far_sib[1].wait_recv()
    split_b(sib_far)
    a_local.wait()

    def c_copy(k):
        return remote(to_send.at[k], arrived.at[k], c_send.at[k], c_recv.at[k], partner)

    def out_copy(k):
        return pltpu.make_async_copy(
            own_part.at[k], out_ref.at[source_col(k, z, x_hi)], out_sem.at[k]
        )

    def terms(i, half):
        for s in range(SLOTS):
            for n in range(2):
                t = table[s, i * 4 + half * 2 + n]
                rhs[0, s * TILE : (s + 1) * TILE, n * TILE : (n + 1) * TILE] = b_hi[t]
                rhs[1, s * TILE : (s + 1) * TILE, n * TILE : (n + 1) * TILE] = b_lo[t]
        both = jnp.dot(lhs[...], rhs[0], preferred_element_type=jnp.float32)
        low = jnp.dot(lhs[0:TILE, :], rhs[1], preferred_element_type=jnp.float32)
        return both[0:TILE] + (both[TILE : 2 * TILE] + low)

    def finish(k):
        c_copy(k).wait_recv()
        own_part[k] = own_part[k] + arrived[k]
        out_copy(k).start()

    @pl.loop(0, 16)
    def _(k):
        @pl.when((k >= 8) & (k < 14))
        def _():
            a_arrival(k).wait_recv()

        @pl.when((k >= 8) & (k < 10))
        def _():
            a_forward(k).start()

        @pl.when((k >= 10) & (k < 14))
        def _():
            a_forward_half(k).start()

        @pl.when(k >= 14)
        def _():
            a_arrival_half(k, 0).wait_recv()
            a_arrival_half(k, 1).wait_recv()

        i = source_col(k, z, x_hi)
        for s in range(SLOTS):
            value = a_all[k, s * TILE : (s + 1) * TILE, :]
            hi = value.astype(jnp.bfloat16)
            lhs[0:TILE, s * TILE : (s + 1) * TILE] = hi
            lhs[TILE : 2 * TILE, s * TILE : (s + 1) * TILE] = (
                value - hi.astype(jnp.float32)
            ).astype(jnp.bfloat16)
        theirs = terms(i, 1 - layer)
        to_send[k, 0] = theirs[:, 0:TILE]
        to_send[k, 1] = theirs[:, TILE : 2 * TILE]
        c_copy(k).start()
        ours = terms(i, layer)
        own_part[k, 0] = ours[:, 0:TILE]
        own_part[k, 1] = ours[:, TILE : 2 * TILE]

        @pl.when(k >= 8)
        def _():
            finish(k - 8)

    @pl.loop(8, 16)
    def _(k):
        finish(k)

    @pl.loop(0, 16)
    def _(k):
        out_copy(k).wait()
        c_copy(k).wait_send()

    for copy in (a_far, a_up, a_down, a_far_up, a_far_down):
        copy.wait_send()

    @pl.loop(2, 10)
    def _(k):
        a_forward(k).wait_send()

    @pl.loop(10, 14)
    def _(k):
        a_forward_half(k).wait_send()

    for copy in (b_own_up, b_own_down, b_own_sib, b_fwd_up, b_fwd_down, b_down_sib, b_up_sib):
        copy.wait_send()
    for copy in b_far_sib:
        copy.wait_send()


def on_device(a_tiles, a_cols, b_tiles, b_rows, c_cols):
    row = lax.axis_index("row")
    a_index = jnp.broadcast_to(
        jnp.pad(a_cols.reshape(SLOTS, 1), ((0, 1), (0, 0)), constant_values=-1), (8, TILE)
    )
    b_index = lax.dynamic_update_slice(
        jnp.full((8, TILE), -5, jnp.int32),
        jnp.broadcast_to(b_rows.reshape(1, B_TILES), (8, B_TILES)),
        (0, row * B_TILES),
    )
    f32, i32, bf16 = jnp.float32, jnp.int32, jnp.bfloat16
    dma = pltpu.SemaphoreType.DMA
    anywhere = pl.BlockSpec(memory_space=pl.ANY)
    in_vmem = pl.BlockSpec(memory_space=pltpu.VMEM)
    out = pl.pallas_call(
        kernel,
        out_shape=jax.ShapeDtypeStruct((16, 2, TILE, TILE), f32),
        in_specs=[pl.BlockSpec(memory_space=pltpu.SMEM), in_vmem, in_vmem, anywhere, anywhere],
        out_specs=anywhere,
        scratch_shapes=[
            pltpu.VMEM((16, A_ROWS, TILE), f32),
            pltpu.VMEM((N_ROW, B_ROWS, TILE), f32),
            pltpu.VMEM((B_ALL + 1, TILE, TILE), bf16),
            pltpu.VMEM((B_ALL + 1, TILE, TILE), bf16),
            pltpu.VMEM((N_COL, 8, TILE), i32),
            pltpu.VMEM((N_ROW, 8, TILE), i32),
            pltpu.VMEM((8, TILE), i32),
            pltpu.SMEM((8, TILE), i32),
            pltpu.VMEM((2 * TILE, A_ROWS), bf16),
            pltpu.VMEM((2, A_ROWS, 2 * TILE), bf16),
            pltpu.VMEM((16, 2, TILE, TILE), f32),
            pltpu.VMEM((16, 2, TILE, TILE), f32),
            pltpu.VMEM((16, 2, TILE, TILE), f32),
            dma((3,)),
            dma((N_COL,)),
            dma((N_COL,)),
            dma((N_ROW,)),
            dma((N_ROW,)),
            dma((17,)),
            dma((18,)),
            dma((9,)),
            dma((9,)),
            dma((16,)),
            dma((16,)),
            dma((16,)),
        ],
        compiler_params=pltpu.CompilerParams(
            collective_id=0, has_side_effects=True, vmem_limit_bytes=48 * 2**20
        ),
        cost_estimate=pl.CostEstimate(
            flops=6 * 16 * 28 * TILE**3, bytes_accessed=4 * 2**20, transcendentals=0
        ),
        name="gather_multiply_sum",
    )(
        c_cols[:, 0, :],
        a_index,
        b_index,
        a_tiles.reshape(A_ROWS, TILE),
        b_tiles.reshape(B_ROWS, TILE),
    )
    return out[:, None]


def solution(mesh):
    return jax.shard_map(
        on_device,
        mesh=mesh,
        in_specs=(
            P(("row", "col"), "layer", None, None, None),
            P(("row", "col"), "layer", None),
            P(("row", "col"), "layer", None, None, None),
            P(("row", "col"), "layer", None),
            P("row", "col", None),
        ),
        out_specs=P("row", "col", "layer", None, None),
        check_vma=False,
    )
```

```python
import jax
import jax.numpy as jnp
from jax import lax
from jax.experimental import pallas as pl
from jax.experimental.pallas import tpu as pltpu
from jax.sharding import PartitionSpec as P

MESH = pl.DeviceIdType.MESH
TILE = 128
SLOTS = 7
A_ROWS = SLOTS * TILE
B_TILES = 2 * SLOTS
B_ROWS = B_TILES * TILE
N_ROW, N_COL = 8, 16
B_ALL = N_ROW * B_TILES
HALF_A = A_ROWS // 2


def source_col(k, z, x_hi):
    distance = (k + 2) // 4
    other = (k // 2 + 1 + (15 - k) // 15 + k // 15) % 2
    sign = 2 * (k % 2) - 1
    return ((z + sign * distance + 8) % 8) * 2 + (x_hi + other) % 2


def kernel(
    want_ref,
    a_cols_ref,
    b_rows_ref,
    a_ref,
    b_ref,
    own_ref,
    arrived_ref,
    a_all,
    b_all,
    b_hi,
    b_lo,
    want,
    a_cols,
    b_rows,
    a_index_all,
    b_index_all,
    a_index_own,
    b_index_own,
    table_vmem,
    table,
    lhs,
    rhs,
    to_send,
    local_sem,
    ai_send,
    ai_recv,
    bi_send,
    bi_recv,
    a_send,
    a_recv,
    b_send,
    b_recv,
    c_send,
    c_recv,
):
    row, col, layer = lax.axis_index("row"), lax.axis_index("col"), lax.axis_index("layer")
    z, x_hi = col // 2, col % 2
    y, core = row // 2, row % 2

    def at(r, c, l):
        return (r, c, l)

    z_up = at(row, (col + 2) % N_COL, layer)
    z_down = at(row, (col + N_COL - 2) % N_COL, layer)
    x_far = at(row, z * 2 + (x_hi + 1) % 2, layer)
    y_up_row, y_down_row, y_far_row = (row + 2) % N_ROW, (row + 6) % N_ROW, (row + 4) % N_ROW
    y_up, y_down = at(y_up_row, col, layer), at(y_down_row, col, layer)
    sibling_row = y * 2 + (core + 1) % 2
    sibling = at(sibling_row, col, layer)
    sib_up, sib_down, sib_far = (
        (sibling_row + 2) % N_ROW,
        (sibling_row + 6) % N_ROW,
        (sibling_row + 4) % N_ROW,
    )
    partner = at(row, col, 1 - layer)

    def remote(src, dst, send_sem, recv_sem, device):
        return pltpu.make_async_remote_copy(
            src_ref=src,
            dst_ref=dst,
            send_sem=send_sem,
            recv_sem=recv_sem,
            device_id=device,
            device_id_type=MESH,
        )

    a_local = pltpu.make_async_copy(a_ref, a_all.at[0], local_sem.at[0])
    b_local = pltpu.make_async_copy(b_ref, b_all.at[row], local_sem.at[1])
    scalars = [
        pltpu.make_async_copy(src, dst, local_sem.at[3 + n])
        for n, (src, dst) in enumerate(
            ((a_cols_ref, a_cols), (b_rows_ref, b_rows), (want_ref, want))
        )
    ]

    barrier = pltpu.get_barrier_semaphore()

    @pl.loop(1, N_COL)
    def _(d):
        pl.semaphore_signal(
            barrier, inc=1, device_id=at(row, (col + d) % N_COL, layer), device_id_type=MESH
        )

    @pl.loop(1, N_ROW)
    def _(d):
        pl.semaphore_signal(
            barrier, inc=1, device_id=at((row + d) % N_ROW, col, layer), device_id_type=MESH
        )

    pl.semaphore_signal(barrier, inc=1, device_id=partner, device_id_type=MESH)
    for copy in scalars:
        copy.start()
    b_local.start()
    a_local.start()
    for copy in scalars:
        copy.wait()
    lane = lax.broadcasted_iota(jnp.int32, (8, TILE), 1)
    sublane = lax.broadcasted_iota(jnp.int32, (8, TILE), 0)
    a_index = jnp.full((8, TILE), -1, jnp.int32)
    for s in range(SLOTS):
        a_index = jnp.where(sublane == s, a_cols[0, 0, s], a_index)
    b_index = jnp.full((8, TILE), -5, jnp.int32)
    for t in range(B_TILES):
        b_index = jnp.where(lane == row * B_TILES + t, b_rows[t // SLOTS, 0, t % SLOTS], b_index)
    a_index_own[...] = a_index
    b_index_own[...] = b_index
    a_index_all[col] = a_index
    b_index_all[row] = b_index
    b_hi[B_ALL] = jnp.zeros((TILE, TILE), jnp.bfloat16)
    b_lo[B_ALL] = jnp.zeros((TILE, TILE), jnp.bfloat16)
    pl.semaphore_wait(barrier, N_COL + N_ROW - 1)

    def a_index_copy(d):
        return remote(
            a_index_own,
            a_index_all.at[col],
            ai_send.at[d],
            ai_recv.at[d],
            at(row, (col + d) % N_COL, layer),
        )

    def b_index_copy(d):
        return remote(
            b_index_own,
            b_index_all.at[row],
            bi_send.at[d],
            bi_recv.at[d],
            at((row + d) % N_ROW, col, layer),
        )

    b_own_up = remote(b_ref, b_all.at[row], b_send.at[0], b_recv.at[0], y_up)
    b_own_down = remote(b_ref, b_all.at[row], b_send.at[1], b_recv.at[1], y_down)
    b_own_sib = remote(b_ref, b_all.at[row], b_send.at[2], b_recv.at[2], sibling)
    b_down_sib = remote(
        b_all.at[y_down_row], b_all.at[y_down_row], b_send.at[3], b_recv.at[3], sibling
    )
    b_up_sib = remote(b_all.at[y_up_row], b_all.at[y_up_row], b_send.at[4], b_recv.at[4], sibling)
    b_pieces = ((0, 4), (7, 4), (4, 3), (11, 3))
    b_forward, b_far_sib = [], []
    for n, (tile, count) in enumerate(b_pieces):
        part = pl.ds(tile * TILE, count * TILE)
        came, goes = (y_down_row, y_up) if n % 2 == 0 else (y_up_row, y_down)
        b_forward.append(
            remote(
                b_all.at[came, part], b_all.at[came, part], b_send.at[5 + n], b_recv.at[5 + n], goes
            )
        )
        b_far_sib.append(
            remote(
                b_all.at[y_far_row, part],
                b_all.at[y_far_row, part],
                b_send.at[9 + n],
                b_recv.at[9 + n],
                sibling,
            )
        )
    b_own_up.start()
    b_own_down.start()

    a_far = remote(a_ref, a_all.at[1], a_send.at[16], a_recv.at[1], x_far)
    a_up = remote(a_ref, a_all.at[2], a_send.at[14], a_recv.at[2], z_up)
    a_down = remote(a_ref, a_all.at[3], a_send.at[15], a_recv.at[3], z_down)
    a_far.start()
    a_up.start()
    a_down.start()
    b_own_sib.start()

    @pl.loop(1, N_ROW)
    def _(d):
        b_index_copy(d).start()

    @pl.loop(1, N_COL)
    def _(d):
        a_index_copy(d).start()

    def split_b(r, first=0, count=B_TILES):
        @pl.loop(first, first + count)
        def _(t):
            value = b_all[r, pl.ds(pl.multiple_of(t * TILE, TILE), TILE), :]
            hi = value.astype(jnp.bfloat16)
            b_hi[r * B_TILES + t] = hi
            b_lo[r * B_TILES + t] = (value - hi.astype(jnp.float32)).astype(jnp.bfloat16)

    def a_forward(k):
        ahead = (col + (1 - k % 2) * 2 + (k % 2) * (N_COL - 2)) % N_COL
        return remote(
            a_all.at[k], a_all.at[k + 4], a_send.at[k], a_recv.at[k + 4], at(row, ahead, layer)
        )

    def a_forward_half(k):
        ahead = (col + (1 - k % 2) * 2 + (k % 2) * (N_COL - 2)) % N_COL
        part = pl.ds(pl.multiple_of((k % 2) * HALF_A, HALF_A), HALF_A)
        return remote(
            a_all.at[k, part],
            a_all.at[14 + (k - 10) // 2, part],
            a_send.at[k],
            a_recv.at[k + 4],
            at(row, ahead, layer),
        )

    a_far_up = remote(a_all.at[1], a_all.at[4], a_send.at[0], a_recv.at[4], z_up)
    a_far_down = remote(a_all.at[1], a_all.at[5], a_send.at[1], a_recv.at[5], z_down)

    def a_arrival(k):
        return remote(a_all.at[k], a_all.at[k], a_send.at[k], a_recv.at[k], z_up)

    def a_arrival_half(k, n):
        part = pl.ds(n * HALF_A, HALF_A)
        return remote(
            a_all.at[k, part],
            a_all.at[k, part],
            a_send.at[k],
            a_recv.at[14 + 2 * (k - 14) + n],
            z_up,
        )

    b_local.wait()
    split_b(row)
    b_own_sib.wait_recv()
    split_b(sibling_row)
    for k in (2, 3):
        a_arrival(k).wait_recv()
        a_forward(k).start()
    @pl.loop(1, N_ROW)
    def _(d):
        b_index_copy(d).wait()

    @pl.loop(1, N_COL)
    def _(d):
        a_index_copy(d).wait()

    b_index = b_index_all[0]
    for r in range(1, N_ROW):
        b_index = jnp.maximum(b_index, b_index_all[r])
    panel = lane // SLOTS

    def one_row(i, found):
        a_index = a_index_all[i]
        for q in range(4):
            wanted = want[q, i]
            wanted_panel = wanted // 32 * 2 + wanted % 2
            match = (a_index == b_index) & (panel == wanted_panel)
            position = jnp.min(jnp.where(match, lane, B_ALL), axis=1, keepdims=True)
            found = jnp.where(lane == i * 4 + q, position, found)
        return found

    table_vmem[...] = lax.fori_loop(
        0, N_COL, one_row, jnp.full((8, TILE), B_ALL, jnp.int32), unroll=4
    )
    to_table = pltpu.make_async_copy(table_vmem, table, local_sem.at[2])
    to_table.start()
    to_table.wait()

    a_arrival(1).wait_recv()
    a_far_up.start()
    a_far_down.start()
    b_own_up.wait_recv()
    b_forward[0].start()
    b_forward[2].start()
    b_down_sib.start()
    b_own_down.wait_recv()
    b_forward[1].start()
    b_forward[3].start()
    b_up_sib.start()
    split_b(y_down_row)
    split_b(y_up_row)
    b_down_sib.wait_recv()
    split_b(sib_down)
    b_up_sib.wait_recv()
    split_b(sib_up)
    for k in (6, 7):
        a_arrival(k).wait_recv()
        a_forward(k).start()
    a_local.wait()
    for n in range(4):
        b_forward[n].wait_recv()
        b_far_sib[n].start()
    for tile, count in b_pieces:
        split_b(y_far_row, tile, count)
    for n, (tile, count) in enumerate(b_pieces):
        b_far_sib[n].wait_recv()
        split_b(sib_far, tile, count)

    def c_copy(k):
        return remote(
            to_send.at[k],
            arrived_ref.at[source_col(k, z, x_hi)],
            c_send.at[k],
            c_recv.at[k],
            partner,
        )

    def terms(i, half):
        for s in range(SLOTS):
            for n in range(2):
                t = table[s, i * 4 + half * 2 + n]
                rhs[0, s * TILE : (s + 1) * TILE, n * TILE : (n + 1) * TILE] = b_hi[t]
                rhs[1, s * TILE : (s + 1) * TILE, n * TILE : (n + 1) * TILE] = b_lo[t]
        both = jnp.dot(lhs[...], rhs[0], preferred_element_type=jnp.float32)
        low = jnp.dot(lhs[0:TILE, :], rhs[1], preferred_element_type=jnp.float32)
        return both[0:TILE] + (both[TILE : 2 * TILE] + low)

    @pl.loop(0, 16)
    def _(k):
        @pl.when(((k >= 4) & (k < 6)) | ((k >= 8) & (k < 14)))
        def _():
            a_arrival(k).wait_recv()

        @pl.when(((k >= 4) & (k < 6)) | ((k >= 8) & (k < 10)))
        def _():
            a_forward(k).start()

        @pl.when((k >= 10) & (k < 14))
        def _():
            a_forward_half(k).start()

        @pl.when(k >= 14)
        def _():
            a_arrival_half(k, 0).wait_recv()
            a_arrival_half(k, 1).wait_recv()

        i = source_col(k, z, x_hi)
        for s in range(SLOTS):
            value = a_all[k, s * TILE : (s + 1) * TILE, :]
            hi = value.astype(jnp.bfloat16)
            lhs[0:TILE, s * TILE : (s + 1) * TILE] = hi
            lhs[TILE : 2 * TILE, s * TILE : (s + 1) * TILE] = (
                value - hi.astype(jnp.float32)
            ).astype(jnp.bfloat16)
        theirs = terms(i, 1 - layer)
        to_send[k, 0] = theirs[:, 0:TILE]
        to_send[k, 1] = theirs[:, TILE : 2 * TILE]
        c_copy(k).start()
        ours = terms(i, layer)
        own_ref[i, 0] = ours[:, 0:TILE]
        own_ref[i, 1] = ours[:, TILE : 2 * TILE]

    for copy in (a_far, a_up, a_down, a_far_up, a_far_down):
        copy.wait_send()

    @pl.loop(2, 10)
    def _(k):
        a_forward(k).wait_send()

    @pl.loop(10, 14)
    def _(k):
        a_forward_half(k).wait_send()

    for copy in (b_own_up, b_own_down, b_own_sib, b_down_sib, b_up_sib, *b_forward, *b_far_sib):
        copy.wait_send()

    @pl.loop(0, 16)
    def _(k):
        c_copy(k).wait()


def on_device(a_tiles, a_cols, b_tiles, b_rows, c_cols):
    f32, i32, bf16 = jnp.float32, jnp.int32, jnp.bfloat16
    dma = pltpu.SemaphoreType.DMA
    in_hbm = pl.BlockSpec(memory_space=pltpu.HBM)
    in_vmem = pl.BlockSpec(memory_space=pltpu.VMEM)
    part = jax.ShapeDtypeStruct((16, 2, TILE, TILE), f32)
    own, arrived = pl.pallas_call(
        kernel,
        out_shape=(part, part),
        in_specs=[in_hbm] * 5,
        out_specs=(in_vmem, in_vmem),
        scratch_shapes=[
            pltpu.VMEM((16, A_ROWS, TILE), f32),
            pltpu.VMEM((N_ROW, B_ROWS, TILE), f32),
            pltpu.VMEM((B_ALL + 1, TILE, TILE), bf16),
            pltpu.VMEM((B_ALL + 1, TILE, TILE), bf16),
            pltpu.SMEM((4, N_COL), i32),
            pltpu.SMEM((1, 1, SLOTS), i32),
            pltpu.SMEM((2, 1, SLOTS), i32),
            pltpu.VMEM((N_COL, 8, TILE), i32),
            pltpu.VMEM((N_ROW, 8, TILE), i32),
            pltpu.VMEM((8, TILE), i32),
            pltpu.VMEM((8, TILE), i32),
            pltpu.VMEM((8, TILE), i32),
            pltpu.SMEM((8, TILE), i32),
            pltpu.VMEM((2 * TILE, A_ROWS), bf16),
            pltpu.VMEM((2, A_ROWS, 2 * TILE), bf16),
            pltpu.VMEM((16, 2, TILE, TILE), f32),
            dma((6,)),
            dma((N_COL,)),
            dma((N_COL,)),
            dma((N_ROW,)),
            dma((N_ROW,)),
            dma((17,)),
            dma((18,)),
            dma((13,)),
            dma((13,)),
            dma((16,)),
            dma((16,)),
        ],
        compiler_params=pltpu.CompilerParams(
            collective_id=0, has_side_effects=True, vmem_limit_bytes=48 * 2**20
        ),
        cost_estimate=pl.CostEstimate(
            flops=6 * 16 * 28 * TILE**3, bytes_accessed=4 * 2**20, transcendentals=0
        ),
        name="gather_multiply_sum",
    )(
        c_cols.reshape(16, 4).T,
        a_cols,
        b_rows,
        a_tiles.reshape(A_ROWS, TILE),
        b_tiles.reshape(B_ROWS, TILE),
    )
    return (own + arrived)[:, None]


def solution(mesh):
    return jax.shard_map(
        on_device,
        mesh=mesh,
        in_specs=(
            P(("row", "col"), "layer", None, None, None),
            P(("row", "col"), "layer", None),
            P(("row", "col"), "layer", None, None, None),
            P(("row", "col"), "layer", None),
            P("row", "col", None),
        ),
        out_specs=P("row", "col", "layer", None, None),
        check_vma=False,
    )
```

```python
import jax
import jax.numpy as jnp
from jax import lax
from jax.experimental import pallas as pl
from jax.experimental.pallas import tpu as pltpu
from jax.sharding import PartitionSpec as P

MESH = pl.DeviceIdType.MESH
TILE = 128
SLOTS = 7
A_ROWS = SLOTS * TILE
B_TILES = 2 * SLOTS
B_ROWS = B_TILES * TILE
N_ROW, N_COL = 8, 16
B_ALL = N_ROW * B_TILES
HALF_A = A_ROWS // 2


def source_col(k, z, x_hi):
    distance = (k + 2) // 4
    other = (k // 2 + 1 + (15 - k) // 15 + k // 15) % 2
    sign = 2 * (k % 2) - 1
    return ((z + sign * distance + 8) % 8) * 2 + (x_hi + other) % 2


def kernel(
    want_ref,
    a_cols_ref,
    b_rows_ref,
    a_ref,
    b_ref,
    own_ref,
    arrived_ref,
    a_all,
    b_all,
    b_hi,
    b_lo,
    want,
    a_cols,
    b_rows,
    a_index_all,
    b_index_all,
    a_index_own,
    b_index_own,
    table_vmem,
    table,
    lhs,
    rhs,
    to_send,
    local_sem,
    ai_send,
    ai_recv,
    bi_send,
    bi_recv,
    a_send,
    a_recv,
    b_send,
    b_recv,
    c_send,
    c_recv,
):
    row, col, layer = lax.axis_index("row"), lax.axis_index("col"), lax.axis_index("layer")
    z, x_hi = col // 2, col % 2
    y, core = row // 2, row % 2

    def at(r, c, l):
        return (r, c, l)

    z_up = at(row, (col + 2) % N_COL, layer)
    z_down = at(row, (col + N_COL - 2) % N_COL, layer)
    x_far = at(row, z * 2 + (x_hi + 1) % 2, layer)
    y_up_row, y_down_row, y_far_row = (row + 2) % N_ROW, (row + 6) % N_ROW, (row + 4) % N_ROW
    y_up, y_down = at(y_up_row, col, layer), at(y_down_row, col, layer)
    sibling_row = y * 2 + (core + 1) % 2
    sibling = at(sibling_row, col, layer)
    sib_up, sib_down, sib_far = (
        (sibling_row + 2) % N_ROW,
        (sibling_row + 6) % N_ROW,
        (sibling_row + 4) % N_ROW,
    )
    partner = at(row, col, 1 - layer)

    def remote(src, dst, send_sem, recv_sem, device):
        return pltpu.make_async_remote_copy(
            src_ref=src,
            dst_ref=dst,
            send_sem=send_sem,
            recv_sem=recv_sem,
            device_id=device,
            device_id_type=MESH,
        )

    a_local = pltpu.make_async_copy(a_ref, a_all.at[0], local_sem.at[0])
    b_local = pltpu.make_async_copy(b_ref, b_all.at[row], local_sem.at[1])
    scalars = [
        pltpu.make_async_copy(src, dst, local_sem.at[3 + n])
        for n, (src, dst) in enumerate(
            ((a_cols_ref, a_cols), (b_rows_ref, b_rows), (want_ref, want))
        )
    ]

    barrier = pltpu.get_barrier_semaphore()

    @pl.loop(1, N_COL)
    def _(d):
        pl.semaphore_signal(
            barrier, inc=1, device_id=at(row, (col + d) % N_COL, layer), device_id_type=MESH
        )

    @pl.loop(1, N_ROW)
    def _(d):
        pl.semaphore_signal(
            barrier, inc=1, device_id=at((row + d) % N_ROW, col, layer), device_id_type=MESH
        )

    pl.semaphore_signal(barrier, inc=1, device_id=partner, device_id_type=MESH)
    for copy in scalars:
        copy.start()
    b_local.start()
    a_local.start()
    pl.semaphore_wait(barrier, N_COL + N_ROW - 1)

    def a_index_copy(d):
        return remote(
            a_index_own,
            a_index_all.at[col],
            ai_send.at[d],
            ai_recv.at[d],
            at(row, (col + d) % N_COL, layer),
        )

    def b_index_copy(d):
        return remote(
            b_index_own,
            b_index_all.at[row],
            bi_send.at[d],
            bi_recv.at[d],
            at((row + d) % N_ROW, col, layer),
        )

    b_own_up = remote(b_ref, b_all.at[row], b_send.at[0], b_recv.at[0], y_up)
    b_own_down = remote(b_ref, b_all.at[row], b_send.at[1], b_recv.at[1], y_down)
    b_own_sib = remote(b_ref, b_all.at[row], b_send.at[2], b_recv.at[2], sibling)
    b_down_sib = remote(
        b_all.at[y_down_row], b_all.at[y_down_row], b_send.at[3], b_recv.at[3], sibling
    )
    b_up_sib = remote(b_all.at[y_up_row], b_all.at[y_up_row], b_send.at[4], b_recv.at[4], sibling)
    b_pieces = ((0, 4), (7, 4), (4, 3), (11, 3))
    b_forward, b_far_sib = [], []
    for n, (tile, count) in enumerate(b_pieces):
        part = pl.ds(tile * TILE, count * TILE)
        came, goes = (y_down_row, y_up) if n % 2 == 0 else (y_up_row, y_down)
        b_forward.append(
            remote(
                b_all.at[came, part], b_all.at[came, part], b_send.at[5 + n], b_recv.at[5 + n], goes
            )
        )
        b_far_sib.append(
            remote(
                b_all.at[y_far_row, part],
                b_all.at[y_far_row, part],
                b_send.at[9 + n],
                b_recv.at[9 + n],
                sibling,
            )
        )
    b_own_up.start()
    b_own_down.start()

    a_far = remote(a_ref, a_all.at[1], a_send.at[16], a_recv.at[1], x_far)
    a_up = remote(a_ref, a_all.at[2], a_send.at[14], a_recv.at[2], z_up)
    a_down = remote(a_ref, a_all.at[3], a_send.at[15], a_recv.at[3], z_down)
    a_far.start()
    a_up.start()
    a_down.start()
    b_own_sib.start()

    for copy in scalars:
        copy.wait()
    lane = lax.broadcasted_iota(jnp.int32, (8, TILE), 1)
    sublane = lax.broadcasted_iota(jnp.int32, (8, TILE), 0)
    a_index = jnp.full((8, TILE), -1, jnp.int32)
    for s in range(SLOTS):
        a_index = jnp.where(sublane == s, a_cols[0, 0, s], a_index)
    b_index = jnp.full((8, TILE), -5, jnp.int32)
    for t in range(B_TILES):
        b_index = jnp.where(lane == row * B_TILES + t, b_rows[t // SLOTS, 0, t % SLOTS], b_index)
    a_index_own[...] = a_index
    b_index_own[...] = b_index
    a_index_all[col] = a_index
    b_index_all[row] = b_index
    b_hi[B_ALL] = jnp.zeros((TILE, TILE), jnp.bfloat16)
    b_lo[B_ALL] = jnp.zeros((TILE, TILE), jnp.bfloat16)

    @pl.loop(1, N_ROW)
    def _(d):
        b_index_copy(d).start()

    @pl.loop(1, N_COL)
    def _(d):
        a_index_copy(d).start()

    def split_b(r, first=0, count=B_TILES):
        @pl.loop(first, first + count)
        def _(t):
            value = b_all[r, pl.ds(pl.multiple_of(t * TILE, TILE), TILE), :]
            hi = value.astype(jnp.bfloat16)
            b_hi[r * B_TILES + t] = hi
            b_lo[r * B_TILES + t] = (value - hi.astype(jnp.float32)).astype(jnp.bfloat16)

    def a_forward(k):
        ahead = (col + (1 - k % 2) * 2 + (k % 2) * (N_COL - 2)) % N_COL
        return remote(
            a_all.at[k], a_all.at[k + 4], a_send.at[k], a_recv.at[k + 4], at(row, ahead, layer)
        )

    def a_forward_half(k):
        ahead = (col + (1 - k % 2) * 2 + (k % 2) * (N_COL - 2)) % N_COL
        part = pl.ds(pl.multiple_of((k % 2) * HALF_A, HALF_A), HALF_A)
        return remote(
            a_all.at[k, part],
            a_all.at[14 + (k - 10) // 2, part],
            a_send.at[k],
            a_recv.at[k + 4],
            at(row, ahead, layer),
        )

    a_far_up = remote(a_all.at[1], a_all.at[4], a_send.at[0], a_recv.at[4], z_up)
    a_far_down = remote(a_all.at[1], a_all.at[5], a_send.at[1], a_recv.at[5], z_down)

    def a_arrival(k):
        return remote(a_all.at[k], a_all.at[k], a_send.at[k], a_recv.at[k], z_up)

    def a_arrival_half(k, n):
        part = pl.ds(n * HALF_A, HALF_A)
        return remote(
            a_all.at[k, part],
            a_all.at[k, part],
            a_send.at[k],
            a_recv.at[14 + 2 * (k - 14) + n],
            z_up,
        )

    b_local.wait()
    split_b(row)
    b_own_sib.wait_recv()
    split_b(sibling_row)
    for k in (2, 3):
        a_arrival(k).wait_recv()
        a_forward(k).start()
    a_arrival(1).wait_recv()
    a_far_up.start()
    a_far_down.start()
    b_own_up.wait_recv()
    b_forward[0].start()
    b_forward[2].start()
    b_down_sib.start()
    b_own_down.wait_recv()
    b_forward[1].start()
    b_forward[3].start()
    b_up_sib.start()
    split_b(y_down_row)
    split_b(y_up_row)
    b_down_sib.wait_recv()
    split_b(sib_down)
    b_up_sib.wait_recv()
    split_b(sib_up)
    for k in (6, 7):
        a_arrival(k).wait_recv()
        a_forward(k).start()
    a_local.wait()
    @pl.loop(1, N_ROW)
    def _(d):
        b_index_copy(d).wait()

    @pl.loop(1, N_COL)
    def _(d):
        a_index_copy(d).wait()

    b_index = b_index_all[0]
    for r in range(1, N_ROW):
        b_index = jnp.maximum(b_index, b_index_all[r])
    panel = lane // SLOTS

    def one_row(i, found):
        a_index = a_index_all[i]
        for q in range(4):
            wanted = want[q, i]
            wanted_panel = wanted // 32 * 2 + wanted % 2
            match = (a_index == b_index) & (panel == wanted_panel)
            position = jnp.min(jnp.where(match, lane, B_ALL), axis=1, keepdims=True)
            found = jnp.where(lane == i * 4 + q, position, found)
        return found

    table_vmem[...] = lax.fori_loop(
        0, N_COL, one_row, jnp.full((8, TILE), B_ALL, jnp.int32), unroll=4
    )
    to_table = pltpu.make_async_copy(table_vmem, table, local_sem.at[2])
    to_table.start()
    to_table.wait()

    for n in range(4):
        b_forward[n].wait_recv()
        b_far_sib[n].start()
    for tile, count in b_pieces:
        split_b(y_far_row, tile, count)
    for n, (tile, count) in enumerate(b_pieces):
        b_far_sib[n].wait_recv()
        split_b(sib_far, tile, count)

    def c_copy(k):
        return remote(
            to_send.at[k],
            arrived_ref.at[source_col(k, z, x_hi)],
            c_send.at[k],
            c_recv.at[k],
            partner,
        )

    def terms(i, half):
        for s in range(SLOTS):
            for n in range(2):
                t = table[s, i * 4 + half * 2 + n]
                rhs[0, s * TILE : (s + 1) * TILE, n * TILE : (n + 1) * TILE] = b_hi[t]
                rhs[1, s * TILE : (s + 1) * TILE, n * TILE : (n + 1) * TILE] = b_lo[t]
        both = jnp.dot(lhs[...], rhs[0], preferred_element_type=jnp.float32)
        low = jnp.dot(lhs[0:TILE, :], rhs[1], preferred_element_type=jnp.float32)
        return both[0:TILE] + (both[TILE : 2 * TILE] + low)

    @pl.loop(0, 16)
    def _(k):
        @pl.when(((k >= 4) & (k < 6)) | ((k >= 8) & (k < 14)))
        def _():
            a_arrival(k).wait_recv()

        @pl.when(((k >= 4) & (k < 6)) | ((k >= 8) & (k < 10)))
        def _():
            a_forward(k).start()

        @pl.when((k >= 10) & (k < 14))
        def _():
            a_forward_half(k).start()

        @pl.when(k >= 14)
        def _():
            a_arrival_half(k, 0).wait_recv()
            a_arrival_half(k, 1).wait_recv()

        i = source_col(k, z, x_hi)
        for s in range(SLOTS):
            value = a_all[k, s * TILE : (s + 1) * TILE, :]
            hi = value.astype(jnp.bfloat16)
            lhs[0:TILE, s * TILE : (s + 1) * TILE] = hi
            lhs[TILE : 2 * TILE, s * TILE : (s + 1) * TILE] = (
                value - hi.astype(jnp.float32)
            ).astype(jnp.bfloat16)
        theirs = terms(i, 1 - layer)
        to_send[k, 0] = theirs[:, 0:TILE]
        to_send[k, 1] = theirs[:, TILE : 2 * TILE]
        c_copy(k).start()
        ours = terms(i, layer)
        own_ref[i, 0] = ours[:, 0:TILE]
        own_ref[i, 1] = ours[:, TILE : 2 * TILE]

    for copy in (a_far, a_up, a_down, a_far_up, a_far_down):
        copy.wait_send()

    @pl.loop(2, 10)
    def _(k):
        a_forward(k).wait_send()

    @pl.loop(10, 14)
    def _(k):
        a_forward_half(k).wait_send()

    for copy in (b_own_up, b_own_down, b_own_sib, b_down_sib, b_up_sib, *b_forward, *b_far_sib):
        copy.wait_send()

    @pl.loop(0, 16)
    def _(k):
        c_copy(k).wait()


def hbm(value):
    return pltpu.with_memory_space_constraint(value, pltpu.HBM)


def on_device(a_tiles, a_cols, b_tiles, b_rows, c_cols):
    f32, i32, bf16 = jnp.float32, jnp.int32, jnp.bfloat16
    dma = pltpu.SemaphoreType.DMA
    in_hbm = pl.BlockSpec(memory_space=pltpu.HBM)
    in_vmem = pl.BlockSpec(memory_space=pltpu.VMEM)
    part = jax.ShapeDtypeStruct((16, 2, TILE, TILE), f32)
    own, arrived = pl.pallas_call(
        kernel,
        out_shape=(part, part),
        in_specs=[in_hbm] * 5,
        out_specs=(in_vmem, in_vmem),
        scratch_shapes=[
            pltpu.VMEM((16, A_ROWS, TILE), f32),
            pltpu.VMEM((N_ROW, B_ROWS, TILE), f32),
            pltpu.VMEM((B_ALL + 1, TILE, TILE), bf16),
            pltpu.VMEM((B_ALL + 1, TILE, TILE), bf16),
            pltpu.SMEM((4, N_COL), i32),
            pltpu.SMEM((1, 1, SLOTS), i32),
            pltpu.SMEM((2, 1, SLOTS), i32),
            pltpu.VMEM((N_COL, 8, TILE), i32),
            pltpu.VMEM((N_ROW, 8, TILE), i32),
            pltpu.VMEM((8, TILE), i32),
            pltpu.VMEM((8, TILE), i32),
            pltpu.VMEM((8, TILE), i32),
            pltpu.SMEM((8, TILE), i32),
            pltpu.VMEM((2 * TILE, A_ROWS), bf16),
            pltpu.VMEM((2, A_ROWS, 2 * TILE), bf16),
            pltpu.VMEM((16, 2, TILE, TILE), f32),
            dma((6,)),
            dma((N_COL,)),
            dma((N_COL,)),
            dma((N_ROW,)),
            dma((N_ROW,)),
            dma((17,)),
            dma((18,)),
            dma((13,)),
            dma((13,)),
            dma((16,)),
            dma((16,)),
        ],
        compiler_params=pltpu.CompilerParams(
            collective_id=0, has_side_effects=True, vmem_limit_bytes=48 * 2**20
        ),
        cost_estimate=pl.CostEstimate(
            flops=6 * 16 * 28 * TILE**3, bytes_accessed=4 * 2**20, transcendentals=0
        ),
        name="gather_multiply_sum",
    )(
        hbm(c_cols.reshape(16, 4).T),
        hbm(a_cols),
        hbm(b_rows),
        hbm(a_tiles.reshape(A_ROWS, TILE)),
        hbm(b_tiles.reshape(B_ROWS, TILE)),
    )
    return (own + arrived)[:, None]


def solution(mesh):
    return jax.shard_map(
        on_device,
        mesh=mesh,
        in_specs=(
            P(("row", "col"), "layer", None, None, None),
            P(("row", "col"), "layer", None),
            P(("row", "col"), "layer", None, None, None),
            P(("row", "col"), "layer", None),
            P("row", "col", None),
        ),
        out_specs=P("row", "col", "layer", None, None),
        check_vma=False,
    )
```

```python
import jax
import jax.numpy as jnp
from jax import lax
from jax.experimental import pallas as pl
from jax.experimental.pallas import tpu as pltpu
from jax.sharding import PartitionSpec as P

MESH = pl.DeviceIdType.MESH
TILE = 128
SLOTS = 7
A_ROWS = SLOTS * TILE
B_TILES = 2 * SLOTS
B_ROWS = B_TILES * TILE
N_ROW, N_COL = 8, 16
B_ALL = N_ROW * B_TILES
HALF_A = A_ROWS // 2
HALF_B = B_ROWS // 2


def source_col(k, z, x_hi):
    distance = (k + 2) // 4
    other = (k // 2 + 1 + (15 - k) // 15 + k // 15) % 2
    sign = 2 * (k % 2) - 1
    return ((z + sign * distance + 8) % 8) * 2 + (x_hi + other) % 2


def kernel(
    want_ref,
    a_cols_ref,
    b_rows_ref,
    a_ref,
    b_ref,
    own_ref,
    arrived_ref,
    a_all,
    b_all,
    b_hi,
    b_lo,
    want,
    a_cols,
    b_rows,
    a_index_all,
    b_index_all,
    b_index_own,
    table_vmem,
    table,
    lhs,
    rhs,
    to_send,
    local_sem,
    table_sem,
    ai_send,
    ai_recv,
    bi_send,
    bi_recv,
    a_send,
    a_recv,
    b_send,
    b_recv,
    c_send,
    c_recv,
):
    row, col, layer = lax.axis_index("row"), lax.axis_index("col"), lax.axis_index("layer")
    z, x_hi = col // 2, col % 2
    y, core = row // 2, row % 2

    def at(r, c, l):
        return (r, c, l)

    z_up = at(row, (col + 2) % N_COL, layer)
    z_down = at(row, (col + N_COL - 2) % N_COL, layer)
    x_far = at(row, z * 2 + (x_hi + 1) % 2, layer)
    y_up_row, y_down_row, y_far_row = (row + 2) % N_ROW, (row + 6) % N_ROW, (row + 4) % N_ROW
    y_up, y_down = at(y_up_row, col, layer), at(y_down_row, col, layer)
    sibling_row = y * 2 + (core + 1) % 2
    sibling = at(sibling_row, col, layer)
    sib_up, sib_down, sib_far = (
        (sibling_row + 2) % N_ROW,
        (sibling_row + 6) % N_ROW,
        (sibling_row + 4) % N_ROW,
    )
    partner = at(row, col, 1 - layer)

    def remote(src, dst, send_sem, recv_sem, device):
        return pltpu.make_async_remote_copy(
            src_ref=src,
            dst_ref=dst,
            send_sem=send_sem,
            recv_sem=recv_sem,
            device_id=device,
            device_id_type=MESH,
        )

    a_local = pltpu.make_async_copy(a_ref, a_all.at[0], local_sem.at[0])
    b_local = pltpu.make_async_copy(b_ref, b_all.at[row], local_sem.at[1])
    scalars = [
        pltpu.make_async_copy(src, dst, local_sem.at[3 + n])
        for n, (src, dst) in enumerate(
            ((a_cols_ref, a_cols), (b_rows_ref, b_rows), (want_ref, want))
        )
    ]

    before = 2 * (z % 2) + x_hi
    barrier = pltpu.get_barrier_semaphore()

    @pl.loop(1, N_ROW)
    def _(d):
        pl.semaphore_signal(
            barrier, inc=1, device_id=at((row + d) % N_ROW, col, layer), device_id_type=MESH
        )

    pl.semaphore_signal(barrier, inc=1, device_id=partner, device_id_type=MESH)
    for copy in scalars:
        copy.start()
    b_local.start()
    a_local.start()
    pl.semaphore_wait(barrier, N_ROW + before)

    halves = (pl.ds(0, HALF_B), pl.ds(HALF_B, HALF_B))

    def b_copy(r, part, n, device):
        return remote(b_all.at[r, part], b_all.at[r, part], b_send.at[n], b_recv.at[n], device)

    def b_own(half, n, device):
        part = halves[half]
        return remote(b_ref.at[part], b_all.at[row, part], b_send.at[n], b_recv.at[n], device)

    b_own_up = [b_own(0, 0, y_up), b_own(1, 1, y_up)]
    b_own_down = [b_own(1, 2, y_down), b_own(0, 3, y_down)]
    b_own_sib = remote(b_ref, b_all.at[row], b_send.at[4], b_recv.at[4], sibling)
    b_down_sib = [b_copy(y_down_row, halves[half], 5 + half, sibling) for half in (0, 1)]
    b_up_sib = [b_copy(y_up_row, halves[half], 8 - half, sibling) for half in (1, 0)]
    b_pieces = ((0, 4), (7, 4), (4, 3), (11, 3))
    b_forward, b_far_sib = [], []
    for n, (tile, count) in enumerate(b_pieces):
        part = pl.ds(tile * TILE, count * TILE)
        came, goes = (y_down_row, y_up) if n % 2 == 0 else (y_up_row, y_down)
        b_forward.append(b_copy(came, part, 9 + n, goes))
        b_far_sib.append(b_copy(y_far_row, part, 13 + n, sibling))
    for n in range(2):
        b_own_up[n].start()
        b_own_down[n].start()
    b_own_sib.start()
    for device in (z_up, z_down, x_far):
        pl.semaphore_signal(barrier, inc=1, device_id=device, device_id_type=MESH)

    def b_index_copy(d):
        return remote(
            b_index_own,
            b_index_all.at[row],
            bi_send.at[d],
            bi_recv.at[d],
            at((row + d) % N_ROW, col, layer),
        )

    for copy in scalars:
        copy.wait()
    lane = lax.broadcasted_iota(jnp.int32, (8, TILE), 1)
    sublane = lax.broadcasted_iota(jnp.int32, (8, TILE), 0)
    a_index = jnp.full((8, TILE), -1, jnp.int32)
    for s in range(SLOTS):
        a_index = jnp.where(sublane == s, a_cols[0, 0, s], a_index)
    b_index = jnp.full((8, TILE), -5, jnp.int32)
    for t in range(B_TILES):
        b_index = jnp.where(lane == row * B_TILES + t, b_rows[t // SLOTS, 0, t % SLOTS], b_index)
    b_index_own[...] = b_index
    b_index_all[row] = b_index
    a_index_all[0] = a_index

    @pl.loop(1, N_ROW)
    def _(d):
        b_index_copy(d).start()

    class Both:
        def __init__(self, *copies):
            self.copies = copies

        def start(self):
            for copy in self.copies:
                copy.start()

        def wait_send(self):
            for copy in self.copies:
                copy.wait_send()

    def a_index_copy(src, dst, n, device):
        return remote(
            a_index_all.at[src], a_index_all.at[dst], ai_send.at[n], ai_recv.at[dst], device
        )

    def a_copy(src, dst, n, device):
        block = a_ref if src == 0 else a_all.at[src]
        return Both(
            a_index_copy(src, dst, n, device),
            remote(block, a_all.at[dst], a_send.at[n], a_recv.at[dst], device),
        )

    a_first = [
        a_copy(0, 2, 14, z_up),
        a_copy(0, 3, 15, z_down),
        a_copy(0, 1, 16, x_far),
    ]
    a_second = [a_copy(1, 4, 0, z_up), a_copy(1, 5, 1, z_down)]

    @pl.when(before < 3)
    def _():
        pl.semaphore_wait(barrier, 3 - before)

    for copy in a_first:
        copy.start()
    b_hi[B_ALL] = jnp.zeros((TILE, TILE), jnp.bfloat16)
    b_lo[B_ALL] = jnp.zeros((TILE, TILE), jnp.bfloat16)

    def split_b(r, first=0, count=B_TILES):
        @pl.loop(first, first + count)
        def _(t):
            value = b_all[r, pl.ds(pl.multiple_of(t * TILE, TILE), TILE), :]
            hi = value.astype(jnp.bfloat16)
            b_hi[r * B_TILES + t] = hi
            b_lo[r * B_TILES + t] = (value - hi.astype(jnp.float32)).astype(jnp.bfloat16)

    def ahead(k):
        return at(row, (col + (1 - k % 2) * 2 + (k % 2) * (N_COL - 2)) % N_COL, layer)

    def a_forward_index(k):
        return a_index_copy(k, k + 4, k, ahead(k))

    def a_forward_index_last(k):
        return a_index_copy(k, 14 + (k - 10) // 2, k, ahead(k))

    def a_forward(k):
        return remote(a_all.at[k], a_all.at[k + 4], a_send.at[k], a_recv.at[k + 4], ahead(k))

    def a_forward_half(k):
        part = pl.ds(pl.multiple_of((k % 2) * HALF_A, HALF_A), HALF_A)
        return remote(
            a_all.at[k, part],
            a_all.at[14 + (k - 10) // 2, part],
            a_send.at[k],
            a_recv.at[k + 4],
            ahead(k),
        )

    def a_index_arrival(k):
        return remote(a_index_all.at[k], a_index_all.at[k], ai_send.at[k], ai_recv.at[k], z_up)

    def a_arrival(k):
        return remote(a_all.at[k], a_all.at[k], a_send.at[k], a_recv.at[k], z_up)

    def a_arrival_half(k, n):
        part = pl.ds(n * HALF_A, HALF_A)
        return remote(
            a_all.at[k, part],
            a_all.at[k, part],
            a_send.at[k],
            a_recv.at[14 + 2 * (k - 14) + n],
            z_up,
        )

    def table_copy(k):
        return pltpu.make_async_copy(table_vmem.at[k], table.at[k], table_sem.at[k])

    def make_table(k):
        b_index = b_index_all[0]
        for r in range(1, N_ROW):
            b_index = jnp.maximum(b_index, b_index_all[r])
        i = source_col(k, z, x_hi)
        a_index = a_index_all[k]
        found = jnp.full((8, TILE), B_ALL, jnp.int32)
        for q in range(4):
            wanted = want[q, i]
            wanted_panel = wanted // 32 * 2 + wanted % 2
            match = (a_index == b_index) & (lane // SLOTS == wanted_panel)
            position = jnp.min(jnp.where(match, lane, B_ALL), axis=1, keepdims=True)
            found = jnp.where(lane == q, position, found)
        table_vmem[k] = found
        table_copy(k).start()

    b_local.wait()
    split_b(row)
    b_own_sib.wait_recv()
    split_b(sibling_row)
    for k in (2, 3):
        a_index_arrival(k).wait_recv()
        a_forward_index(k).start()
        a_arrival(k).wait_recv()
        a_forward(k).start()
    b_own_up[0].wait_recv()
    b_forward[0].start()
    b_forward[2].start()
    b_own_down[0].wait_recv()
    b_forward[1].start()
    b_forward[3].start()
    b_down_sib[0].start()
    b_up_sib[0].start()
    b_own_up[1].wait_recv()
    b_down_sib[1].start()
    b_own_down[1].wait_recv()
    b_up_sib[1].start()
    a_index_arrival(1).wait_recv()
    a_arrival(1).wait_recv()
    for copy in a_second:
        copy.start()
    split_b(y_down_row)
    split_b(y_up_row)
    b_down_sib[0].wait_recv()
    b_down_sib[1].wait_recv()
    split_b(sib_down)
    b_up_sib[0].wait_recv()
    b_up_sib[1].wait_recv()
    split_b(sib_up)

    @pl.loop(1, N_ROW)
    def _(d):
        b_index_copy(d).wait()

    @pl.loop(0, 4)
    def _(k):
        make_table(k)

    a_local.wait()
    for n in range(4):
        b_forward[n].wait_recv()
        b_far_sib[n].start()

    @pl.loop(6, 8)
    def _(k):
        a_index_arrival(k).wait_recv()
        a_forward_index(k).start()
        a_arrival(k).wait_recv()
        a_forward(k).start()
        make_table(k)

    for tile, count in b_pieces:
        split_b(y_far_row, tile, count)
    for n, (tile, count) in enumerate(b_pieces):
        b_far_sib[n].wait_recv()
        split_b(sib_far, tile, count)

    def c_copy(k):
        return remote(
            to_send.at[k],
            arrived_ref.at[source_col(k, z, x_hi)],
            c_send.at[k],
            c_recv.at[k],
            partner,
        )

    def terms(k, half):
        for s in range(SLOTS):
            for n in range(2):
                t = table[k, s, half * 2 + n]
                rhs[0, s * TILE : (s + 1) * TILE, n * TILE : (n + 1) * TILE] = b_hi[t]
                rhs[1, s * TILE : (s + 1) * TILE, n * TILE : (n + 1) * TILE] = b_lo[t]
        both = jnp.dot(lhs[...], rhs[0], preferred_element_type=jnp.float32)
        low = jnp.dot(lhs[0:TILE, :], rhs[1], preferred_element_type=jnp.float32)
        return both[0:TILE] + (both[TILE : 2 * TILE] + low)

    @pl.loop(0, 16)
    def _(k):
        full = ((k >= 4) & (k < 6)) | ((k >= 8) & (k < 10))
        half = (k >= 10) & (k < 14)
        late = ((k >= 4) & (k < 6)) | (k >= 8)

        @pl.when(late)
        def _():
            a_index_arrival(k).wait_recv()

        @pl.when(full)
        def _():
            a_forward_index(k).start()

        @pl.when(half & (k % 2 == 0))
        def _():
            a_forward_index_last(k).start()

        @pl.when(late)
        def _():
            make_table(k)

        @pl.when(full | half)
        def _():
            a_arrival(k).wait_recv()

        @pl.when(full)
        def _():
            a_forward(k).start()

        @pl.when(half)
        def _():
            a_forward_half(k).start()

        @pl.when(k >= 14)
        def _():
            a_arrival_half(k, 0).wait_recv()
            a_arrival_half(k, 1).wait_recv()

        i = source_col(k, z, x_hi)
        for s in range(SLOTS):
            value = a_all[k, s * TILE : (s + 1) * TILE, :]
            hi = value.astype(jnp.bfloat16)
            lhs[0:TILE, s * TILE : (s + 1) * TILE] = hi
            lhs[TILE : 2 * TILE, s * TILE : (s + 1) * TILE] = (
                value - hi.astype(jnp.float32)
            ).astype(jnp.bfloat16)
        table_copy(k).wait()
        theirs = terms(k, 1 - layer)
        to_send[k, 0] = theirs[:, 0:TILE]
        to_send[k, 1] = theirs[:, TILE : 2 * TILE]
        c_copy(k).start()
        ours = terms(k, layer)
        own_ref[i, 0] = ours[:, 0:TILE]
        own_ref[i, 1] = ours[:, TILE : 2 * TILE]

    for copy in (*a_first, *a_second):
        copy.wait_send()

    @pl.loop(2, 10)
    def _(k):
        a_forward_index(k).wait_send()
        a_forward(k).wait_send()

    @pl.loop(10, 14)
    def _(k):
        @pl.when(k % 2 == 0)
        def _():
            a_forward_index_last(k).wait_send()

        a_forward_half(k).wait_send()

    for copy in (*b_own_up, *b_own_down, b_own_sib, *b_down_sib, *b_up_sib, *b_forward, *b_far_sib):
        copy.wait_send()

    @pl.loop(0, 16)
    def _(k):
        c_copy(k).wait()


def hbm(value):
    return pltpu.with_memory_space_constraint(value, pltpu.HBM)


def on_device(a_tiles, a_cols, b_tiles, b_rows, c_cols):
    f32, i32, bf16 = jnp.float32, jnp.int32, jnp.bfloat16
    dma = pltpu.SemaphoreType.DMA
    in_hbm = pl.BlockSpec(memory_space=pltpu.HBM)
    in_vmem = pl.BlockSpec(memory_space=pltpu.VMEM)
    part = jax.ShapeDtypeStruct((16, 2, TILE, TILE), f32)
    own, arrived = pl.pallas_call(
        kernel,
        out_shape=(part, part),
        in_specs=[in_hbm] * 5,
        out_specs=(in_vmem, in_vmem),
        scratch_shapes=[
            pltpu.VMEM((16, A_ROWS, TILE), f32),
            pltpu.VMEM((N_ROW, B_ROWS, TILE), f32),
            pltpu.VMEM((B_ALL + 1, TILE, TILE), bf16),
            pltpu.VMEM((B_ALL + 1, TILE, TILE), bf16),
            pltpu.SMEM((4, N_COL), i32),
            pltpu.SMEM((1, 1, SLOTS), i32),
            pltpu.SMEM((2, 1, SLOTS), i32),
            pltpu.VMEM((16, 8, TILE), i32),
            pltpu.VMEM((N_ROW, 8, TILE), i32),
            pltpu.VMEM((8, TILE), i32),
            pltpu.VMEM((16, 8, TILE), i32),
            pltpu.SMEM((16, 8, TILE), i32),
            pltpu.VMEM((2 * TILE, A_ROWS), bf16),
            pltpu.VMEM((2, A_ROWS, 2 * TILE), bf16),
            pltpu.VMEM((16, 2, TILE, TILE), f32),
            dma((6,)),
            dma((16,)),
            dma((17,)),
            dma((16,)),
            dma((N_ROW,)),
            dma((N_ROW,)),
            dma((17,)),
            dma((18,)),
            dma((17,)),
            dma((17,)),
            dma((16,)),
            dma((16,)),
        ],
        compiler_params=pltpu.CompilerParams(
            collective_id=0, has_side_effects=True, vmem_limit_bytes=48 * 2**20
        ),
        cost_estimate=pl.CostEstimate(
            flops=6 * 16 * 28 * TILE**3, bytes_accessed=4 * 2**20, transcendentals=0
        ),
        name="gather_multiply_sum",
    )(
        hbm(c_cols.reshape(16, 4).T),
        hbm(a_cols),
        hbm(b_rows),
        hbm(a_tiles.reshape(A_ROWS, TILE)),
        hbm(b_tiles.reshape(B_ROWS, TILE)),
    )
    return (own + arrived)[:, None]


def solution(mesh):
    return jax.shard_map(
        on_device,
        mesh=mesh,
        in_specs=(
            P(("row", "col"), "layer", None, None, None),
            P(("row", "col"), "layer", None),
            P(("row", "col"), "layer", None, None, None),
            P(("row", "col"), "layer", None),
            P("row", "col", None),
        ),
        out_specs=P("row", "col", "layer", None, None),
        check_vma=False,
    )
```

```python
import jax
import jax.numpy as jnp
from jax import lax
from jax.experimental import pallas as pl
from jax.experimental.pallas import tpu as pltpu
from jax.sharding import PartitionSpec as P

MESH = pl.DeviceIdType.MESH
TILE = 128
SLOTS = 7
A_ROWS = SLOTS * TILE
B_TILES = 2 * SLOTS
B_ROWS = B_TILES * TILE
N_ROW, N_COL = 8, 16
B_ALL = N_ROW * B_TILES
HALF_A = A_ROWS // 2
HALF_B = B_ROWS // 2


def source_col(k, z, x_hi):
    distance = (k + 2) // 4
    other = (k // 2 + 1 + (15 - k) // 15 + k // 15) % 2
    sign = 2 * (k % 2) - 1
    return ((z + sign * distance + 8) % 8) * 2 + (x_hi + other) % 2


def slot_of(n):
    m = n % 4
    third, fourth = (n // 8) * (1 - n // 12), n // 12
    return n + third * (2 - 4 * (m // 2)) + fourth * (2 - 3 * ((m + 3) // 4) + m // 3)


def kernel(
    want_ref,
    a_cols_ref,
    b_rows_ref,
    a_ref,
    b_ref,
    own_ref,
    arrived_ref,
    a_all,
    b_all,
    b_hi,
    b_lo,
    want,
    a_cols,
    b_rows,
    a_index_all,
    b_index_all,
    b_index_own,
    table_vmem,
    table,
    lhs,
    rhs,
    to_send,
    local_sem,
    table_sem,
    ai_send,
    ai_recv,
    bi_send,
    bi_recv,
    a_send,
    a_recv,
    b_send,
    b_recv,
    c_send,
    c_recv,
):
    row, col, layer = lax.axis_index("row"), lax.axis_index("col"), lax.axis_index("layer")
    z, x_hi = col // 2, col % 2
    y, core = row // 2, row % 2

    def at(r, c, l):
        return (r, c, l)

    z_up = at(row, (col + 2) % N_COL, layer)
    z_down = at(row, (col + N_COL - 2) % N_COL, layer)
    x_far = at(row, z * 2 + (x_hi + 1) % 2, layer)
    y_up_row, y_down_row, y_far_row = (row + 2) % N_ROW, (row + 6) % N_ROW, (row + 4) % N_ROW
    y_up, y_down = at(y_up_row, col, layer), at(y_down_row, col, layer)
    sibling_row = y * 2 + (core + 1) % 2
    sibling = at(sibling_row, col, layer)
    sib_up, sib_down, sib_far = (
        (sibling_row + 2) % N_ROW,
        (sibling_row + 6) % N_ROW,
        (sibling_row + 4) % N_ROW,
    )
    partner = at(row, col, 1 - layer)

    def remote(src, dst, send_sem, recv_sem, device):
        return pltpu.make_async_remote_copy(
            src_ref=src,
            dst_ref=dst,
            send_sem=send_sem,
            recv_sem=recv_sem,
            device_id=device,
            device_id_type=MESH,
        )

    a_local = pltpu.make_async_copy(a_ref, a_all.at[0], local_sem.at[0])
    b_local = pltpu.make_async_copy(b_ref, b_all.at[row], local_sem.at[1])
    scalars = [
        pltpu.make_async_copy(src, dst, local_sem.at[3 + n])
        for n, (src, dst) in enumerate(
            ((a_cols_ref, a_cols), (b_rows_ref, b_rows), (want_ref, want))
        )
    ]

    before = (z + 7) // 8 + (z // 5) * (1 - z // 6) + x_hi
    barrier = pltpu.get_barrier_semaphore()

    @pl.loop(1, N_ROW)
    def _(d):
        pl.semaphore_signal(
            barrier, inc=1, device_id=at((row + d) % N_ROW, col, layer), device_id_type=MESH
        )

    pl.semaphore_signal(barrier, inc=1, device_id=partner, device_id_type=MESH)
    for copy in scalars:
        copy.start()
    b_local.start()
    a_local.start()
    pl.semaphore_wait(barrier, N_ROW + before)

    halves = (pl.ds(0, HALF_B), pl.ds(HALF_B, HALF_B))

    def b_copy(r, part, n, device):
        return remote(b_all.at[r, part], b_all.at[r, part], b_send.at[n], b_recv.at[n], device)

    def b_own(half, n, device):
        part = halves[half]
        return remote(b_ref.at[part], b_all.at[row, part], b_send.at[n], b_recv.at[n], device)

    b_own_up = [b_own(0, 0, y_up), b_own(1, 1, y_up)]
    b_own_down = [b_own(1, 2, y_down), b_own(0, 3, y_down)]
    b_own_sib = remote(b_ref, b_all.at[row], b_send.at[4], b_recv.at[4], sibling)
    b_down_sib = [b_copy(y_down_row, halves[half], 5 + half, sibling) for half in (0, 1)]
    b_up_sib = [b_copy(y_up_row, halves[half], 8 - half, sibling) for half in (1, 0)]
    b_pieces = ((0, 3), (7, 3), (3, 2), (10, 2), (5, 1), (12, 1), (6, 1), (13, 1))
    b_forward, b_far_sib = [], []
    for n, (tile, count) in enumerate(b_pieces):
        part = pl.ds(tile * TILE, count * TILE)
        came, goes = (y_down_row, y_up) if n % 2 == 0 else (y_up_row, y_down)
        b_forward.append(b_copy(came, part, 9 + n, goes))
        b_far_sib.append(b_copy(y_far_row, part, 17 + n, sibling))
    for n in range(2):
        b_own_up[n].start()
        b_own_down[n].start()
    b_own_sib.start()
    for device in (z_up, z_down, x_far):
        pl.semaphore_signal(barrier, inc=1, device_id=device, device_id_type=MESH)

    def b_index_copy(d):
        return remote(
            b_index_own,
            b_index_all.at[row],
            bi_send.at[d],
            bi_recv.at[d],
            at((row + d) % N_ROW, col, layer),
        )

    for copy in scalars:
        copy.wait()
    lane = lax.broadcasted_iota(jnp.int32, (8, TILE), 1)
    sublane = lax.broadcasted_iota(jnp.int32, (8, TILE), 0)
    a_index = jnp.full((8, TILE), -1, jnp.int32)
    for s in range(SLOTS):
        a_index = jnp.where(sublane == s, a_cols[0, 0, s], a_index)
    b_index = jnp.full((8, TILE), -5, jnp.int32)
    for t in range(B_TILES):
        b_index = jnp.where(lane == row * B_TILES + t, b_rows[t // SLOTS, 0, t % SLOTS], b_index)
    b_index_own[...] = b_index
    b_index_all[row] = b_index
    a_index_all[0] = a_index

    @pl.loop(1, N_ROW)
    def _(d):
        b_index_copy(d).start()

    class Both:
        def __init__(self, *copies):
            self.copies = copies

        def start(self):
            for copy in self.copies:
                copy.start()

        def wait_send(self):
            for copy in self.copies:
                copy.wait_send()

    def a_index_copy(src, dst, n, device):
        return remote(
            a_index_all.at[src], a_index_all.at[dst], ai_send.at[n], ai_recv.at[dst], device
        )

    def a_copy(src, dst, n, device):
        block = a_ref if src == 0 else a_all.at[src]
        return Both(
            a_index_copy(src, dst, n, device),
            remote(block, a_all.at[dst], a_send.at[n], a_recv.at[dst], device),
        )

    a_first = [
        a_copy(0, 2, 14, z_up),
        a_copy(0, 3, 15, z_down),
        a_copy(0, 1, 16, x_far),
    ]
    a_second = [a_copy(1, 4, 0, z_up), a_copy(3, 5, 1, x_far)]

    @pl.when(before < 3)
    def _():
        pl.semaphore_wait(barrier, 3 - before)

    for copy in a_first:
        copy.start()
    b_hi[B_ALL] = jnp.zeros((TILE, TILE), jnp.bfloat16)
    b_lo[B_ALL] = jnp.zeros((TILE, TILE), jnp.bfloat16)

    def split_b(r, first=0, count=B_TILES):
        @pl.loop(first, first + count)
        def _(t):
            value = b_all[r, pl.ds(pl.multiple_of(t * TILE, TILE), TILE), :]
            hi = value.astype(jnp.bfloat16)
            b_hi[r * B_TILES + t] = hi
            b_lo[r * B_TILES + t] = (value - hi.astype(jnp.float32)).astype(jnp.bfloat16)

    def ahead(k):
        return at(row, (col + (1 - k % 2) * 2 + (k % 2) * (N_COL - 2)) % N_COL, layer)

    def a_forward_index(k):
        return a_index_copy(k, k + 4, k, ahead(k))

    def a_forward_index_last(k):
        return a_index_copy(k, 14 + (k - 10) // 2, k, ahead(k))

    def a_forward(k):
        return remote(a_all.at[k], a_all.at[k + 4], a_send.at[k], a_recv.at[k + 4], ahead(k))

    def a_forward_last():
        return remote(a_all.at[11], a_all.at[14], a_send.at[11], a_recv.at[14], ahead(11))

    def a_forward_half(k):
        part = pl.ds(pl.multiple_of((k % 2) * HALF_A, HALF_A), HALF_A)
        return remote(
            a_all.at[k, part], a_all.at[15, part], a_send.at[k], a_recv.at[k + 3], ahead(k)
        )

    def a_index_arrival(k):
        return remote(a_index_all.at[k], a_index_all.at[k], ai_send.at[k], ai_recv.at[k], z_up)

    def a_arrival(k):
        return remote(a_all.at[k], a_all.at[k], a_send.at[k], a_recv.at[k], z_up)

    def a_arrival_half(n):
        part = pl.ds(n * HALF_A, HALF_A)
        return remote(
            a_all.at[15, part], a_all.at[15, part], a_send.at[15], a_recv.at[15 + n], z_up
        )

    def table_copy(k):
        return pltpu.make_async_copy(table_vmem.at[k], table.at[k], table_sem.at[k])

    def make_table(k):
        b_index = b_index_all[0]
        for r in range(1, N_ROW):
            b_index = jnp.maximum(b_index, b_index_all[r])
        i = source_col(k, z, x_hi)
        a_index = a_index_all[k]
        found = jnp.full((8, TILE), B_ALL, jnp.int32)
        for q in range(4):
            wanted = want[q, i]
            wanted_panel = wanted // 32 * 2 + wanted % 2
            match = (a_index == b_index) & (lane // SLOTS == wanted_panel)
            position = jnp.min(jnp.where(match, lane, B_ALL), axis=1, keepdims=True)
            found = jnp.where(lane == q, position, found)
        table_vmem[k] = found
        table_copy(k).start()

    b_local.wait()
    split_b(row)
    b_own_sib.wait_recv()
    split_b(sibling_row)
    for k in (2, 3):
        a_index_arrival(k).wait_recv()
        a_forward_index(k).start()
        a_arrival(k).wait_recv()
        a_forward(k).start()
    a_second[1].start()
    b_own_up[0].wait_recv()
    for copy in b_forward[0::2]:
        copy.start()
    b_own_down[0].wait_recv()
    for copy in b_forward[1::2]:
        copy.start()
    a_index_arrival(1).wait_recv()
    a_arrival(1).wait_recv()
    a_second[0].start()
    b_down_sib[0].start()
    b_up_sib[0].start()
    b_own_up[1].wait_recv()
    b_down_sib[1].start()
    b_own_down[1].wait_recv()
    b_up_sib[1].start()
    split_b(y_down_row)
    split_b(y_up_row)

    @pl.loop(6, 8)
    def _(k):
        a_index_arrival(k).wait_recv()
        a_forward_index(k).start()
        a_arrival(k).wait_recv()
        a_forward(k).start()

    b_down_sib[0].wait_recv()
    b_down_sib[1].wait_recv()
    split_b(sib_down)
    b_up_sib[0].wait_recv()
    b_up_sib[1].wait_recv()
    split_b(sib_up)

    @pl.loop(1, N_ROW)
    def _(d):
        b_index_copy(d).wait()

    @pl.loop(0, 4)
    def _(k):
        make_table(k)

    a_local.wait()
    for n in range(len(b_pieces)):
        b_forward[n].wait_recv()
        b_far_sib[n].start()

    for tile, count in b_pieces:
        split_b(y_far_row, tile, count)
    for n, (tile, count) in enumerate(b_pieces):
        b_far_sib[n].wait_recv()
        split_b(sib_far, tile, count)

    def c_copy(k):
        return remote(
            to_send.at[k],
            arrived_ref.at[source_col(k, z, x_hi)],
            c_send.at[k],
            c_recv.at[k],
            partner,
        )

    def terms(k, half):
        for s in range(SLOTS):
            for n in range(2):
                t = table[k, s, half * 2 + n]
                rhs[0, s * TILE : (s + 1) * TILE, n * TILE : (n + 1) * TILE] = b_hi[t]
                rhs[1, s * TILE : (s + 1) * TILE, n * TILE : (n + 1) * TILE] = b_lo[t]
        both = jnp.dot(lhs[...], rhs[0], preferred_element_type=jnp.float32)
        low = jnp.dot(lhs[0:TILE, :], rhs[1], preferred_element_type=jnp.float32)
        return both[0:TILE] + (both[TILE : 2 * TILE] + low)

    @pl.loop(0, 16)
    def _(n):
        k = slot_of(n)

        @pl.when((n == 2) | (n == 10))
        def _():
            for j in (4, 5):
                first = j + n // 10 * 4
                a_arrival(first).wait_recv()
                a_forward(first).start()

        @pl.when(n == 6)
        def _():
            a_arrival(11).wait_recv()
            a_forward_last().start()
            a_arrival(10).wait_recv()

        @pl.when(k == 14)
        def _():
            a_arrival(14).wait_recv()

        @pl.when(k == 12)
        def _():
            for j in (12, 13):
                a_arrival(j).wait_recv()
                a_forward_half(j).start()

        @pl.when(k == 15)
        def _():
            a_arrival_half(0).wait_recv()
            a_arrival_half(1).wait_recv()

        i = source_col(k, z, x_hi)
        for s in range(SLOTS):
            value = a_all[k, s * TILE : (s + 1) * TILE, :]
            hi = value.astype(jnp.bfloat16)
            lhs[0:TILE, s * TILE : (s + 1) * TILE] = hi
            lhs[TILE : 2 * TILE, s * TILE : (s + 1) * TILE] = (
                value - hi.astype(jnp.float32)
            ).astype(jnp.bfloat16)
        table_copy(k).wait()
        theirs = terms(k, 1 - layer)
        to_send[k, 0] = theirs[:, 0:TILE]
        to_send[k, 1] = theirs[:, TILE : 2 * TILE]
        c_copy(k).start()

        soon = slot_of(n + 1)

        @pl.when((soon < 16) & ((soon >= 8) | ((soon >= 4) & (soon < 6))))
        def _():
            a_index_arrival(soon).wait_recv()

        @pl.when(((soon >= 4) & (soon < 6)) | ((soon >= 8) & (soon < 10)))
        def _():
            a_forward_index(soon).start()

        @pl.when((soon == 11) | (soon == 12))
        def _():
            a_forward_index_last(soon).start()

        @pl.when((soon >= 4) & (soon < 16))
        def _():
            make_table(soon)

        ours = terms(k, layer)
        own_ref[i, 0] = ours[:, 0:TILE]
        own_ref[i, 1] = ours[:, TILE : 2 * TILE]

    for copy in (*a_first, *a_second):
        copy.wait_send()

    @pl.loop(2, 10)
    def _(k):
        a_forward_index(k).wait_send()
        a_forward(k).wait_send()

    a_forward_index_last(11).wait_send()
    a_forward_index_last(12).wait_send()
    a_forward_last().wait_send()
    a_forward_half(12).wait_send()
    a_forward_half(13).wait_send()
    for copy in (*b_own_up, *b_own_down, b_own_sib, *b_down_sib, *b_up_sib, *b_forward, *b_far_sib):
        copy.wait_send()

    @pl.loop(0, 16)
    def _(k):
        c_copy(k).wait()


def hbm(value):
    return pltpu.with_memory_space_constraint(value, pltpu.HBM)


def on_device(a_tiles, a_cols, b_tiles, b_rows, c_cols):
    f32, i32, bf16 = jnp.float32, jnp.int32, jnp.bfloat16
    dma = pltpu.SemaphoreType.DMA
    in_hbm = pl.BlockSpec(memory_space=pltpu.HBM)
    in_vmem = pl.BlockSpec(memory_space=pltpu.VMEM)
    part = jax.ShapeDtypeStruct((16, 2, TILE, TILE), f32)
    own, arrived = pl.pallas_call(
        kernel,
        out_shape=(part, part),
        in_specs=[in_hbm] * 5,
        out_specs=(in_vmem, in_vmem),
        scratch_shapes=[
            pltpu.VMEM((16, A_ROWS, TILE), f32),
            pltpu.VMEM((N_ROW, B_ROWS, TILE), f32),
            pltpu.VMEM((B_ALL + 1, TILE, TILE), bf16),
            pltpu.VMEM((B_ALL + 1, TILE, TILE), bf16),
            pltpu.SMEM((4, N_COL), i32),
            pltpu.SMEM((1, 1, SLOTS), i32),
            pltpu.SMEM((2, 1, SLOTS), i32),
            pltpu.VMEM((16, 8, TILE), i32),
            pltpu.VMEM((N_ROW, 8, TILE), i32),
            pltpu.VMEM((8, TILE), i32),
            pltpu.VMEM((16, 8, TILE), i32),
            pltpu.SMEM((16, 8, TILE), i32),
            pltpu.VMEM((2 * TILE, A_ROWS), bf16),
            pltpu.VMEM((2, A_ROWS, 2 * TILE), bf16),
            pltpu.VMEM((16, 2, TILE, TILE), f32),
            dma((6,)),
            dma((16,)),
            dma((17,)),
            dma((16,)),
            dma((N_ROW,)),
            dma((N_ROW,)),
            dma((17,)),
            dma((18,)),
            dma((25,)),
            dma((25,)),
            dma((16,)),
            dma((16,)),
        ],
        compiler_params=pltpu.CompilerParams(
            collective_id=0, has_side_effects=True, vmem_limit_bytes=48 * 2**20
        ),
        cost_estimate=pl.CostEstimate(
            flops=6 * 16 * 28 * TILE**3, bytes_accessed=4 * 2**20, transcendentals=0
        ),
        name="gather_multiply_sum",
    )(
        hbm(c_cols.reshape(16, 4).T),
        hbm(a_cols),
        hbm(b_rows),
        hbm(a_tiles.reshape(A_ROWS, TILE)),
        hbm(b_tiles.reshape(B_ROWS, TILE)),
    )
    return (own + arrived)[:, None]


def solution(mesh):
    return jax.shard_map(
        on_device,
        mesh=mesh,
        in_specs=(
            P(("row", "col"), "layer", None, None, None),
            P(("row", "col"), "layer", None),
            P(("row", "col"), "layer", None, None, None),
            P(("row", "col"), "layer", None),
            P("row", "col", None),
        ),
        out_specs=P("row", "col", "layer", None, None),
        check_vma=False,
    )
```

```python
import jax
import jax.numpy as jnp
from jax import lax
from jax.experimental import pallas as pl
from jax.experimental.pallas import tpu as pltpu
from jax.sharding import PartitionSpec as P

MESH = pl.DeviceIdType.MESH
TILE = 128
SLOTS = 7
A_ROWS = SLOTS * TILE
B_TILES = 2 * SLOTS
B_ROWS = B_TILES * TILE
N_ROW, N_COL = 8, 16
B_ALL = N_ROW * B_TILES
HALF_A = A_ROWS // 2
HALF_B = B_ROWS // 2


def source_col(k, z, x_hi):
    distance = (k + 2) // 4
    other = (k // 2 + 1 + (15 - k) // 15 + k // 15) % 2
    sign = 2 * (k % 2) - 1
    return ((z + sign * distance + 8) % 8) * 2 + (x_hi + other) % 2


def slot_of(n):
    m = n % 4
    third, fourth = (n // 8) * (1 - n // 12), n // 12
    return n + third * (2 - 4 * (m // 2)) + fourth * (2 - 3 * ((m + 3) // 4) + m // 3)


def kernel(
    want_ref,
    a_cols_ref,
    b_rows_ref,
    a_ref,
    b_ref,
    own_ref,
    arrived_ref,
    a_all,
    b_all,
    b_hi,
    b_lo,
    want,
    a_cols,
    b_rows,
    a_index_all,
    b_index_all,
    b_index_own,
    table_vmem,
    table,
    lhs,
    rhs,
    to_send,
    local_sem,
    table_sem,
    ai_send,
    ai_recv,
    bi_send,
    bi_recv,
    a_send,
    a_recv,
    b_send,
    b_recv,
    c_send,
    c_recv,
):
    row, col, layer = lax.axis_index("row"), lax.axis_index("col"), lax.axis_index("layer")
    z, x_hi = col // 2, col % 2
    y, core = row // 2, row % 2

    def at(r, c, l):
        return (r, c, l)

    z_up = at(row, (col + 2) % N_COL, layer)
    z_down = at(row, (col + N_COL - 2) % N_COL, layer)
    x_far = at(row, z * 2 + (x_hi + 1) % 2, layer)
    y_up_row, y_down_row, y_far_row = (row + 2) % N_ROW, (row + 6) % N_ROW, (row + 4) % N_ROW
    y_up, y_down = at(y_up_row, col, layer), at(y_down_row, col, layer)
    sibling_row = y * 2 + (core + 1) % 2
    sibling = at(sibling_row, col, layer)
    sib_up, sib_down, sib_far = (
        (sibling_row + 2) % N_ROW,
        (sibling_row + 6) % N_ROW,
        (sibling_row + 4) % N_ROW,
    )
    partner = at(row, col, 1 - layer)

    def remote(src, dst, send_sem, recv_sem, device):
        return pltpu.make_async_remote_copy(
            src_ref=src,
            dst_ref=dst,
            send_sem=send_sem,
            recv_sem=recv_sem,
            device_id=device,
            device_id_type=MESH,
        )

    a_local = pltpu.make_async_copy(a_ref, a_all.at[0], local_sem.at[0])
    b_local = pltpu.make_async_copy(b_ref, b_all.at[row], local_sem.at[1])
    scalars = [
        pltpu.make_async_copy(src, dst, local_sem.at[3 + n])
        for n, (src, dst) in enumerate(
            ((a_cols_ref, a_cols), (b_rows_ref, b_rows), (want_ref, want))
        )
    ]

    is_4, is_5, is_6 = ((z // v) * (1 - z // (v + 1)) for v in (4, 5, 6))
    before = (z + 7) // 8 + is_4 - is_5 + is_6 + x_hi
    barrier = pltpu.get_barrier_semaphore()

    @pl.loop(1, N_ROW)
    def _(d):
        pl.semaphore_signal(
            barrier, inc=1, device_id=at((row + d) % N_ROW, col, layer), device_id_type=MESH
        )

    pl.semaphore_signal(barrier, inc=1, device_id=partner, device_id_type=MESH)
    for copy in scalars:
        copy.start()
    b_local.start()
    a_local.start()
    pl.semaphore_wait(barrier, N_ROW + before)

    halves = (pl.ds(0, HALF_B), pl.ds(HALF_B, HALF_B))

    def b_copy(r, part, n, device):
        return remote(b_all.at[r, part], b_all.at[r, part], b_send.at[n], b_recv.at[n], device)

    def b_own(half, n, device):
        part = halves[half]
        return remote(b_ref.at[part], b_all.at[row, part], b_send.at[n], b_recv.at[n], device)

    b_own_up = [b_own(0, 0, y_up), b_own(1, 1, y_up)]
    b_own_down = [b_own(1, 2, y_down), b_own(0, 3, y_down)]
    b_own_sib = remote(b_ref, b_all.at[row], b_send.at[4], b_recv.at[4], sibling)
    b_down_sib = [b_copy(y_down_row, halves[half], 5 + half, sibling) for half in (0, 1)]
    b_up_sib = [b_copy(y_up_row, halves[half], 8 - half, sibling) for half in (1, 0)]
    b_pieces = ((0, 3), (7, 3), (3, 2), (10, 2), (5, 1), (12, 1), (6, 1), (13, 1))
    b_forward, b_far_sib = [], []
    for n, (tile, count) in enumerate(b_pieces):
        part = pl.ds(tile * TILE, count * TILE)
        came, goes = (y_down_row, y_up) if n % 2 == 0 else (y_up_row, y_down)
        b_forward.append(b_copy(came, part, 9 + n, goes))
        b_far_sib.append(b_copy(y_far_row, part, 17 + n, sibling))
    for n in range(2):
        b_own_up[n].start()
        b_own_down[n].start()
    b_own_sib.start()
    for device in (z_up, z_down, x_far):
        pl.semaphore_signal(barrier, inc=1, device_id=device, device_id_type=MESH)

    def b_index_copy(d):
        return remote(
            b_index_own,
            b_index_all.at[row],
            bi_send.at[d],
            bi_recv.at[d],
            at((row + d) % N_ROW, col, layer),
        )

    for copy in scalars:
        copy.wait()
    lane = lax.broadcasted_iota(jnp.int32, (8, TILE), 1)
    sublane = lax.broadcasted_iota(jnp.int32, (8, TILE), 0)
    a_index = jnp.full((8, TILE), -1, jnp.int32)
    for s in range(SLOTS):
        a_index = jnp.where(sublane == s, a_cols[0, 0, s], a_index)
    b_index = jnp.full((8, TILE), -5, jnp.int32)
    for t in range(B_TILES):
        b_index = jnp.where(lane == row * B_TILES + t, b_rows[t // SLOTS, 0, t % SLOTS], b_index)
    b_index_own[...] = b_index
    b_index_all[row] = b_index
    a_index_all[0] = a_index

    @pl.loop(1, N_ROW)
    def _(d):
        b_index_copy(d).start()

    class Both:
        def __init__(self, *copies):
            self.copies = copies

        def start(self):
            for copy in self.copies:
                copy.start()

        def wait_send(self):
            for copy in self.copies:
                copy.wait_send()

    def a_index_copy(src, dst, n, device):
        return remote(
            a_index_all.at[src], a_index_all.at[dst], ai_send.at[n], ai_recv.at[dst], device
        )

    def a_copy(src, dst, n, device):
        block = a_ref if src == 0 else a_all.at[src]
        return Both(
            a_index_copy(src, dst, n, device),
            remote(block, a_all.at[dst], a_send.at[n], a_recv.at[dst], device),
        )

    a_first = [
        a_copy(0, 2, 14, z_up),
        a_copy(0, 3, 15, z_down),
        a_copy(0, 1, 16, x_far),
    ]
    a_second = [a_copy(1, 4, 0, z_up), a_copy(3, 5, 1, x_far)]

    @pl.when(before < 3)
    def _():
        pl.semaphore_wait(barrier, 3 - before)

    for copy in a_first:
        copy.start()
    b_hi[B_ALL] = jnp.zeros((TILE, TILE), jnp.bfloat16)
    b_lo[B_ALL] = jnp.zeros((TILE, TILE), jnp.bfloat16)

    def split_b(r, first=0, count=B_TILES):
        @pl.loop(first, first + count)
        def _(t):
            value = b_all[r, pl.ds(pl.multiple_of(t * TILE, TILE), TILE), :]
            hi = value.astype(jnp.bfloat16)
            b_hi[r * B_TILES + t] = hi
            b_lo[r * B_TILES + t] = (value - hi.astype(jnp.float32)).astype(jnp.bfloat16)

    def ahead(k):
        return at(row, (col + (1 - k % 2) * 2 + (k % 2) * (N_COL - 2)) % N_COL, layer)

    def a_forward_index(k):
        return a_index_copy(k, k + 4, k, ahead(k))

    def a_forward_index_last(k):
        return a_index_copy(k, 14 + (k - 10) // 2, k, ahead(k))

    def a_forward(k):
        return remote(a_all.at[k], a_all.at[k + 4], a_send.at[k], a_recv.at[k + 4], ahead(k))

    def a_forward_last():
        return remote(a_all.at[11], a_all.at[14], a_send.at[11], a_recv.at[14], ahead(11))

    def a_forward_half(k):
        part = pl.ds(pl.multiple_of((k % 2) * HALF_A, HALF_A), HALF_A)
        return remote(
            a_all.at[k, part], a_all.at[15, part], a_send.at[k], a_recv.at[k + 3], ahead(k)
        )

    def a_index_arrival(k):
        return remote(a_index_all.at[k], a_index_all.at[k], ai_send.at[k], ai_recv.at[k], z_up)

    def a_arrival(k):
        return remote(a_all.at[k], a_all.at[k], a_send.at[k], a_recv.at[k], z_up)

    def a_arrival_half(n):
        part = pl.ds(n * HALF_A, HALF_A)
        return remote(
            a_all.at[15, part], a_all.at[15, part], a_send.at[15], a_recv.at[15 + n], z_up
        )

    def load_block(n):
        k = slot_of(n)

        @pl.when(n == 2)
        def _():
            a_arrival(4).wait_recv()
            a_forward(4).start()

        @pl.when(n == 10)
        def _():
            for j in (8, 9):
                a_arrival(j).wait_recv()
                a_forward(j).start()

        @pl.when(n == 6)
        def _():
            a_arrival(11).wait_recv()
            a_forward_last().start()
            a_arrival(10).wait_recv()

        @pl.when(k == 14)
        def _():
            a_arrival(14).wait_recv()

        @pl.when(k == 12)
        def _():
            for j in (12, 13):
                a_arrival(j).wait_recv()
                a_forward_half(j).start()

        @pl.when(k == 15)
        def _():
            a_arrival_half(0).wait_recv()
            a_arrival_half(1).wait_recv()

        for s in range(SLOTS):
            value = a_all[k, s * TILE : (s + 1) * TILE, :]
            hi = value.astype(jnp.bfloat16)
            lhs[0:TILE, s * TILE : (s + 1) * TILE] = hi
            lhs[TILE : 2 * TILE, s * TILE : (s + 1) * TILE] = (
                value - hi.astype(jnp.float32)
            ).astype(jnp.bfloat16)

    def table_copy(k):
        return pltpu.make_async_copy(table_vmem.at[k], table.at[k], table_sem.at[k])

    def make_table(k):
        b_index = b_index_all[0]
        for r in range(1, N_ROW):
            b_index = jnp.maximum(b_index, b_index_all[r])
        i = source_col(k, z, x_hi)
        a_index = a_index_all[k]
        found = jnp.full((8, TILE), B_ALL, jnp.int32)
        for q in range(4):
            wanted = want[q, i]
            wanted_panel = wanted // 32 * 2 + wanted % 2
            match = (a_index == b_index) & (lane // SLOTS == wanted_panel)
            position = jnp.min(jnp.where(match, lane, B_ALL), axis=1, keepdims=True)
            found = jnp.where(lane == q, position, found)
        table_vmem[k] = found
        table_copy(k).start()

    b_local.wait()
    split_b(row)
    b_own_sib.wait_recv()
    split_b(sibling_row)
    for k in (2, 3):
        a_index_arrival(k).wait_recv()
        a_forward_index(k).start()
        a_arrival(k).wait_recv()
        a_forward(k).start()
    a_second[1].start()
    b_own_up[0].wait_recv()
    for copy in b_forward[0::2]:
        copy.start()
    b_own_down[0].wait_recv()
    for copy in b_forward[1::2]:
        copy.start()
    a_index_arrival(1).wait_recv()
    a_arrival(1).wait_recv()
    a_second[0].start()
    b_down_sib[0].start()
    b_up_sib[0].start()
    b_own_up[1].wait_recv()
    b_down_sib[1].start()
    b_own_down[1].wait_recv()
    b_up_sib[1].start()
    split_b(y_down_row)
    split_b(y_up_row)

    @pl.loop(6, 8)
    def _(k):
        a_index_arrival(k).wait_recv()
        a_forward_index(k).start()
        a_arrival(k).wait_recv()
        a_forward(k).start()

    b_down_sib[0].wait_recv()
    b_down_sib[1].wait_recv()
    split_b(sib_down)
    b_up_sib[0].wait_recv()
    b_up_sib[1].wait_recv()
    split_b(sib_up)

    @pl.loop(1, N_ROW)
    def _(d):
        b_index_copy(d).wait()

    @pl.loop(0, 4)
    def _(k):
        make_table(k)

    a_index_arrival(5).wait_recv()
    a_forward_index(5).start()
    a_arrival(5).wait_recv()
    a_forward(5).start()
    a_local.wait()
    load_block(0)
    for n in range(len(b_pieces)):
        b_forward[n].wait_recv()
        b_far_sib[n].start()

    for tile, count in b_pieces:
        split_b(y_far_row, tile, count)
    for n, (tile, count) in enumerate(b_pieces):
        b_far_sib[n].wait_recv()
        split_b(sib_far, tile, count)

    def c_copy(k):
        return remote(
            to_send.at[k],
            arrived_ref.at[source_col(k, z, x_hi)],
            c_send.at[k],
            c_recv.at[k],
            partner,
        )

    def terms(k, half):
        for s in range(SLOTS):
            for n in range(2):
                t = table[k, s, half * 2 + n]
                rhs[0, s * TILE : (s + 1) * TILE, n * TILE : (n + 1) * TILE] = b_hi[t]
                rhs[1, s * TILE : (s + 1) * TILE, n * TILE : (n + 1) * TILE] = b_lo[t]
        both = jnp.dot(lhs[...], rhs[0], preferred_element_type=jnp.float32)
        low = jnp.dot(lhs[0:TILE, :], rhs[1], preferred_element_type=jnp.float32)
        return both[0:TILE] + (both[TILE : 2 * TILE] + low)

    @pl.loop(0, 16)
    def _(n):
        k = slot_of(n)
        i = source_col(k, z, x_hi)
        table_copy(k).wait()
        theirs = terms(k, 1 - layer)
        to_send[k, 0] = theirs[:, 0:TILE]
        to_send[k, 1] = theirs[:, TILE : 2 * TILE]
        c_copy(k).start()

        soon = slot_of(n + 1)

        @pl.when((soon == 4) | ((soon >= 8) & (soon < 16)))
        def _():
            a_index_arrival(soon).wait_recv()

        @pl.when((soon == 4) | (soon == 8) | (soon == 9))
        def _():
            a_forward_index(soon).start()

        @pl.when((soon == 11) | (soon == 12))
        def _():
            a_forward_index_last(soon).start()

        @pl.when((soon >= 4) & (soon < 16))
        def _():
            make_table(soon)

        ours = terms(k, layer)
        own_ref[i, 0] = ours[:, 0:TILE]
        own_ref[i, 1] = ours[:, TILE : 2 * TILE]

        @pl.when(n < 15)
        def _():
            load_block(n + 1)

    for copy in (*a_first, *a_second):
        copy.wait_send()

    @pl.loop(2, 10)
    def _(k):
        a_forward_index(k).wait_send()
        a_forward(k).wait_send()

    a_forward_index_last(11).wait_send()
    a_forward_index_last(12).wait_send()
    a_forward_last().wait_send()
    a_forward_half(12).wait_send()
    a_forward_half(13).wait_send()
    for copy in (*b_own_up, *b_own_down, b_own_sib, *b_down_sib, *b_up_sib, *b_forward, *b_far_sib):
        copy.wait_send()

    @pl.loop(0, 16)
    def _(k):
        c_copy(k).wait()


def add_kernel(own_ref, arrived_ref, out_ref, total, sem):
    copies = []
    for n in range(4):
        part = pl.ds(4 * n, 4)
        total[part] = own_ref[part] + arrived_ref[part]
        copies.append(pltpu.make_async_copy(total.at[part], out_ref.at[part], sem.at[n]))
        copies[-1].start()
    for copy in copies:
        copy.wait()


def hbm(value):
    return pltpu.with_memory_space_constraint(value, pltpu.HBM)


def on_device(a_tiles, a_cols, b_tiles, b_rows, c_cols):
    f32, i32, bf16 = jnp.float32, jnp.int32, jnp.bfloat16
    dma = pltpu.SemaphoreType.DMA
    in_hbm = pl.BlockSpec(memory_space=pltpu.HBM)
    in_vmem = pl.BlockSpec(memory_space=pltpu.VMEM)
    part = jax.ShapeDtypeStruct((16, 2, TILE, TILE), f32)
    own, arrived = pl.pallas_call(
        kernel,
        out_shape=(part, part),
        in_specs=[in_hbm] * 5,
        out_specs=(in_vmem, in_vmem),
        scratch_shapes=[
            pltpu.VMEM((16, A_ROWS, TILE), f32),
            pltpu.VMEM((N_ROW, B_ROWS, TILE), f32),
            pltpu.VMEM((B_ALL + 1, TILE, TILE), bf16),
            pltpu.VMEM((B_ALL + 1, TILE, TILE), bf16),
            pltpu.SMEM((4, N_COL), i32),
            pltpu.SMEM((1, 1, SLOTS), i32),
            pltpu.SMEM((2, 1, SLOTS), i32),
            pltpu.VMEM((16, 8, TILE), i32),
            pltpu.VMEM((N_ROW, 8, TILE), i32),
            pltpu.VMEM((8, TILE), i32),
            pltpu.VMEM((16, 8, TILE), i32),
            pltpu.SMEM((16, 8, TILE), i32),
            pltpu.VMEM((2 * TILE, A_ROWS), bf16),
            pltpu.VMEM((2, A_ROWS, 2 * TILE), bf16),
            pltpu.VMEM((16, 2, TILE, TILE), f32),
            dma((6,)),
            dma((16,)),
            dma((17,)),
            dma((16,)),
            dma((N_ROW,)),
            dma((N_ROW,)),
            dma((17,)),
            dma((18,)),
            dma((25,)),
            dma((25,)),
            dma((16,)),
            dma((16,)),
        ],
        compiler_params=pltpu.CompilerParams(
            collective_id=0, has_side_effects=True, vmem_limit_bytes=48 * 2**20
        ),
        cost_estimate=pl.CostEstimate(
            flops=6 * 16 * 28 * TILE**3, bytes_accessed=4 * 2**20, transcendentals=0
        ),
        name="gather_multiply_sum",
    )(
        hbm(c_cols.reshape(16, 4).T),
        hbm(a_cols),
        hbm(b_rows),
        hbm(a_tiles.reshape(A_ROWS, TILE)),
        hbm(b_tiles.reshape(B_ROWS, TILE)),
    )
    out = pl.pallas_call(
        add_kernel,
        out_shape=part,
        in_specs=[in_vmem, in_vmem],
        out_specs=in_hbm,
        scratch_shapes=[pltpu.VMEM((16, 2, TILE, TILE), f32), dma((4,))],
        compiler_params=pltpu.CompilerParams(vmem_limit_bytes=8 * 2**20),
        name="add_halves",
    )(own, arrived)
    return out[:, None]


def solution(mesh):
    return jax.shard_map(
        on_device,
        mesh=mesh,
        in_specs=(
            P(("row", "col"), "layer", None, None, None),
            P(("row", "col"), "layer", None),
            P(("row", "col"), "layer", None, None, None),
            P(("row", "col"), "layer", None),
            P("row", "col", None),
        ),
        out_specs=P("row", "col", "layer", None, None),
        check_vma=False,
    )
```

```python
import jax
import jax.numpy as jnp
from jax import lax
from jax.experimental import pallas as pl
from jax.experimental.pallas import tpu as pltpu
from jax.sharding import PartitionSpec as P

MESH = pl.DeviceIdType.MESH
TILE = 128
SLOTS = 7
A_ROWS = SLOTS * TILE
B_TILES = 2 * SLOTS
B_ROWS = B_TILES * TILE
N_ROW, N_COL = 8, 16
B_ALL = N_ROW * B_TILES
HALF_A = A_ROWS // 2
HALF_B = B_ROWS // 2


def source_col(k, z, x_hi):
    distance = (k + 2) // 4
    other = (k // 2 + 1 + (15 - k) // 15 + k // 15) % 2
    sign = 2 * (k % 2) - 1
    return ((z + sign * distance + 8) % 8) * 2 + (x_hi + other) % 2


def slot_of(n):
    m = n % 4
    third, fourth = (n // 8) * (1 - n // 12), n // 12
    return n + third * (2 - 4 * (m // 2)) + fourth * (2 - 3 * ((m + 3) // 4) + m // 3)


def kernel(
    want_ref,
    a_cols_ref,
    b_rows_ref,
    a_ref,
    b_ref,
    own_ref,
    arrived_ref,
    a_all,
    b_all,
    b_hi,
    b_lo,
    want,
    a_cols,
    b_rows,
    a_index_all,
    b_index_all,
    b_index_own,
    table_vmem,
    table,
    lhs,
    rhs,
    to_send,
    local_sem,
    table_sem,
    ai_send,
    ai_recv,
    bi_send,
    bi_recv,
    a_send,
    a_recv,
    b_send,
    b_recv,
    c_send,
    c_recv,
    answers,
):
    row, col, layer = lax.axis_index("row"), lax.axis_index("col"), lax.axis_index("layer")
    z, x_hi = col // 2, col % 2
    y, core = row // 2, row % 2

    def at(r, c, l):
        return (r, c, l)

    z_up = at(row, (col + 2) % N_COL, layer)
    z_down = at(row, (col + N_COL - 2) % N_COL, layer)
    x_far = at(row, z * 2 + (x_hi + 1) % 2, layer)
    y_up_row, y_down_row, y_far_row = (row + 2) % N_ROW, (row + 6) % N_ROW, (row + 4) % N_ROW
    y_up, y_down = at(y_up_row, col, layer), at(y_down_row, col, layer)
    sibling_row = y * 2 + (core + 1) % 2
    sibling = at(sibling_row, col, layer)
    sib_up, sib_down, sib_far = (
        (sibling_row + 2) % N_ROW,
        (sibling_row + 6) % N_ROW,
        (sibling_row + 4) % N_ROW,
    )
    partner = at(row, col, 1 - layer)

    def remote(src, dst, send_sem, recv_sem, device):
        return pltpu.make_async_remote_copy(
            src_ref=src,
            dst_ref=dst,
            send_sem=send_sem,
            recv_sem=recv_sem,
            device_id=device,
            device_id_type=MESH,
        )

    a_local = pltpu.make_async_copy(a_ref, a_all.at[0], local_sem.at[0])
    b_local = pltpu.make_async_copy(b_ref, b_all.at[row], local_sem.at[1])
    scalars = [
        pltpu.make_async_copy(src, dst, local_sem.at[3 + n])
        for n, (src, dst) in enumerate(
            ((a_cols_ref, a_cols), (b_rows_ref, b_rows), (want_ref, want))
        )
    ]

    other = (core + 1) % 2
    pairs = (
        (z_up, (z < 4) | (z == 5)),
        (z_down, (z == 0) | (z == 5) | (z == 7)),
        (x_far, x_hi == 0),
        (partner, layer == 0),
        (at(y_far_row, col, layer), y < 2),
        (at((y + 2) % 4 * 2 + other, col, layer), y < 2),
        (at((y + 1) % 4 * 2 + other, col, layer), y < 3),
        (at((y + 3) % 4 * 2 + other, col, layer), y == 0),
    )
    is_0, is_4, is_5, is_6 = (
        (z + 8 - v) // 8 * (1 - (z + 7 - v) // 8) for v in (0, 4, 5, 6)
    )
    before = 1 - is_0 + is_4 - is_5 + is_6 + x_hi + layer + 2 * (y // 2) + (y + 1) // 2
    after = len(pairs) - before
    barrier = pltpu.get_barrier_semaphore()
    for device in (y_up, y_down, sibling):
        pl.semaphore_signal(barrier, inc=1, device_id=device, device_id_type=MESH)
    for device, first in pairs:

        @pl.when(first)
        def _():
            pl.semaphore_signal(barrier, inc=1, device_id=device, device_id_type=MESH)

    for copy in scalars:
        copy.start()
    b_local.start()
    a_local.start()
    pl.semaphore_wait(barrier, 3 + before)

    halves = (pl.ds(0, HALF_B), pl.ds(HALF_B, HALF_B))

    def b_copy(r, part, n, device):
        return remote(b_all.at[r, part], b_all.at[r, part], b_send.at[n], b_recv.at[n], device)

    def b_own(half, n, device):
        part = halves[half]
        return remote(b_ref.at[part], b_all.at[row, part], b_send.at[n], b_recv.at[n], device)

    b_own_up = [b_own(0, 0, y_up), b_own(1, 1, y_up)]
    b_own_down = [b_own(1, 2, y_down), b_own(0, 3, y_down)]
    b_own_sib = remote(b_ref, b_all.at[row], b_send.at[4], b_recv.at[4], sibling)
    b_down_sib = [b_copy(y_down_row, halves[half], 5 + half, sibling) for half in (0, 1)]
    b_up_sib = [b_copy(y_up_row, halves[half], 8 - half, sibling) for half in (1, 0)]
    b_pieces = ((0, 3), (7, 3), (3, 2), (10, 2), (5, 1), (12, 1), (6, 1), (13, 1))
    b_forward, b_far_sib = [], []
    for n, (tile, count) in enumerate(b_pieces):
        part = pl.ds(tile * TILE, count * TILE)
        came, goes = (y_down_row, y_up) if n % 2 == 0 else (y_up_row, y_down)
        b_forward.append(b_copy(came, part, 9 + n, goes))
        b_far_sib.append(b_copy(y_far_row, part, 17 + n, sibling))
    for n in range(2):
        b_own_up[n].start()
        b_own_down[n].start()
    b_own_sib.start()
    for device, first in pairs:

        @pl.when(jnp.logical_not(first))
        def _():
            pl.semaphore_signal(answers, inc=1, device_id=device, device_id_type=MESH)


    def b_index_copy(d):
        return remote(
            b_index_own,
            b_index_all.at[row],
            bi_send.at[d],
            bi_recv.at[d],
            at((row + d) % N_ROW, col, layer),
        )

    for copy in scalars:
        copy.wait()
    lane = lax.broadcasted_iota(jnp.int32, (8, TILE), 1)
    sublane = lax.broadcasted_iota(jnp.int32, (8, TILE), 0)
    a_index = jnp.full((8, TILE), -1, jnp.int32)
    for s in range(SLOTS):
        a_index = jnp.where(sublane == s, a_cols[0, 0, s], a_index)
    b_index = jnp.full((8, TILE), -5, jnp.int32)
    for t in range(B_TILES):
        b_index = jnp.where(lane == row * B_TILES + t, b_rows[t // SLOTS, 0, t % SLOTS], b_index)
    b_index_own[...] = b_index
    b_index_all[row] = b_index
    a_index_all[0] = a_index

    class Both:
        def __init__(self, *copies):
            self.copies = copies

        def start(self):
            for copy in self.copies:
                copy.start()

        def wait_send(self):
            for copy in self.copies:
                copy.wait_send()

    def a_index_copy(src, dst, n, device):
        return remote(
            a_index_all.at[src], a_index_all.at[dst], ai_send.at[n], ai_recv.at[dst], device
        )

    def a_copy(src, dst, n, device):
        block = a_ref if src == 0 else a_all.at[src]
        return Both(
            a_index_copy(src, dst, n, device),
            remote(block, a_all.at[dst], a_send.at[n], a_recv.at[dst], device),
        )

    a_first = [
        a_copy(0, 2, 14, z_up),
        a_copy(0, 3, 15, z_down),
        a_copy(0, 1, 16, x_far),
    ]
    a_second = [a_copy(1, 4, 0, z_up), a_copy(3, 5, 1, x_far)]

    @pl.when(after > 0)
    def _():
        pl.semaphore_wait(answers, after)

    for copy in a_first:
        copy.start()

    @pl.loop(1, N_ROW)
    def _(d):
        b_index_copy(d).start()

    b_hi[B_ALL] = jnp.zeros((TILE, TILE), jnp.bfloat16)
    b_lo[B_ALL] = jnp.zeros((TILE, TILE), jnp.bfloat16)

    def split_b(r, first=0, count=B_TILES):
        @pl.loop(first, first + count)
        def _(t):
            value = b_all[r, pl.ds(pl.multiple_of(t * TILE, TILE), TILE), :]
            hi = value.astype(jnp.bfloat16)
            b_hi[r * B_TILES + t] = hi
            b_lo[r * B_TILES + t] = (value - hi.astype(jnp.float32)).astype(jnp.bfloat16)

    def ahead(k):
        return at(row, (col + (1 - k % 2) * 2 + (k % 2) * (N_COL - 2)) % N_COL, layer)

    def a_forward_index(k):
        return a_index_copy(k, k + 4, k, ahead(k))

    def a_forward_index_last(k):
        return a_index_copy(k, 14 + (k - 10) // 2, k, ahead(k))

    def a_forward(k):
        return remote(a_all.at[k], a_all.at[k + 4], a_send.at[k], a_recv.at[k + 4], ahead(k))

    def a_forward_last():
        return remote(a_all.at[11], a_all.at[14], a_send.at[11], a_recv.at[14], ahead(11))

    def a_forward_half(k):
        part = pl.ds(pl.multiple_of((k % 2) * HALF_A, HALF_A), HALF_A)
        return remote(
            a_all.at[k, part], a_all.at[15, part], a_send.at[k], a_recv.at[k + 3], ahead(k)
        )

    def a_index_arrival(k):
        return remote(a_index_all.at[k], a_index_all.at[k], ai_send.at[k], ai_recv.at[k], z_up)

    def a_arrival(k):
        return remote(a_all.at[k], a_all.at[k], a_send.at[k], a_recv.at[k], z_up)

    def a_arrival_half(n):
        part = pl.ds(n * HALF_A, HALF_A)
        return remote(
            a_all.at[15, part], a_all.at[15, part], a_send.at[15], a_recv.at[15 + n], z_up
        )

    def load_block(n):
        k = slot_of(n)

        @pl.when(n == 2)
        def _():
            a_arrival(4).wait_recv()
            a_forward(4).start()

        @pl.when(n == 10)
        def _():
            for j in (8, 9):
                a_arrival(j).wait_recv()
                a_forward(j).start()

        @pl.when(n == 6)
        def _():
            a_arrival(11).wait_recv()
            a_forward_last().start()
            a_arrival(10).wait_recv()

        @pl.when(k == 14)
        def _():
            a_arrival(14).wait_recv()

        @pl.when(k == 12)
        def _():
            for j in (12, 13):
                a_arrival(j).wait_recv()
                a_forward_half(j).start()

        @pl.when(k == 15)
        def _():
            a_arrival_half(0).wait_recv()
            a_arrival_half(1).wait_recv()

        for s in range(SLOTS):
            value = a_all[k, s * TILE : (s + 1) * TILE, :]
            hi = value.astype(jnp.bfloat16)
            lhs[0:TILE, s * TILE : (s + 1) * TILE] = hi
            lhs[TILE : 2 * TILE, s * TILE : (s + 1) * TILE] = (
                value - hi.astype(jnp.float32)
            ).astype(jnp.bfloat16)

    def table_copy(k):
        return pltpu.make_async_copy(table_vmem.at[k], table.at[k], table_sem.at[k])

    def make_table(k):
        b_index = b_index_all[0]
        for r in range(1, N_ROW):
            b_index = jnp.maximum(b_index, b_index_all[r])
        i = source_col(k, z, x_hi)
        a_index = a_index_all[k]
        found = jnp.full((8, TILE), B_ALL, jnp.int32)
        for q in range(4):
            wanted = want[q, i]
            wanted_panel = wanted // 32 * 2 + wanted % 2
            match = (a_index == b_index) & (lane // SLOTS == wanted_panel)
            position = jnp.min(jnp.where(match, lane, B_ALL), axis=1, keepdims=True)
            found = jnp.where(lane == q, position, found)
        table_vmem[k] = found
        table_copy(k).start()

    b_local.wait()
    split_b(row)
    b_own_sib.wait_recv()
    split_b(sibling_row)
    for k in (3, 2):
        a_index_arrival(k).wait_recv()
        a_forward_index(k).start()
        a_arrival(k).wait_recv()
        a_forward(k).start()
        if k == 3:
            a_second[1].start()
    b_own_up[0].wait_recv()
    for copy in b_forward[0::2]:
        copy.start()
    b_own_down[0].wait_recv()
    for copy in b_forward[1::2]:
        copy.start()
    a_index_arrival(1).wait_recv()
    a_arrival(1).wait_recv()
    a_second[0].start()
    b_down_sib[0].start()
    b_up_sib[0].start()
    b_own_up[1].wait_recv()
    b_down_sib[1].start()
    b_own_down[1].wait_recv()
    b_up_sib[1].start()
    split_b(y_down_row)
    split_b(y_up_row)

    @pl.loop(6, 8)
    def _(k):
        a_index_arrival(k).wait_recv()
        a_forward_index(k).start()
        a_arrival(k).wait_recv()
        a_forward(k).start()

    b_down_sib[0].wait_recv()
    b_down_sib[1].wait_recv()
    split_b(sib_down)
    b_up_sib[0].wait_recv()
    b_up_sib[1].wait_recv()
    split_b(sib_up)

    @pl.loop(1, N_ROW)
    def _(d):
        b_index_copy(d).wait()

    @pl.loop(0, 4)
    def _(k):
        make_table(k)

    a_index_arrival(5).wait_recv()
    a_forward_index(5).start()
    a_arrival(5).wait_recv()
    a_forward(5).start()
    a_local.wait()
    load_block(0)
    for n in range(len(b_pieces)):
        b_forward[n].wait_recv()
        b_far_sib[n].start()

    for tile, count in b_pieces:
        split_b(y_far_row, tile, count)
    for n, (tile, count) in enumerate(b_pieces):
        b_far_sib[n].wait_recv()
        split_b(sib_far, tile, count)

    def c_copy(k):
        return remote(
            to_send.at[k],
            arrived_ref.at[source_col(k, z, x_hi)],
            c_send.at[k],
            c_recv.at[k],
            partner,
        )

    def terms(k, half):
        for s in range(SLOTS):
            for n in range(2):
                t = table[k, s, half * 2 + n]
                rhs[0, s * TILE : (s + 1) * TILE, n * TILE : (n + 1) * TILE] = b_hi[t]
                rhs[1, s * TILE : (s + 1) * TILE, n * TILE : (n + 1) * TILE] = b_lo[t]
        both = jnp.dot(lhs[...], rhs[0], preferred_element_type=jnp.float32)
        low = jnp.dot(lhs[0:TILE, :], rhs[1], preferred_element_type=jnp.float32)
        return both[0:TILE] + (both[TILE : 2 * TILE] + low)

    @pl.loop(0, 16)
    def _(n):
        k = slot_of(n)
        i = source_col(k, z, x_hi)
        table_copy(k).wait()
        theirs = terms(k, 1 - layer)
        to_send[k, 0] = theirs[:, 0:TILE]
        to_send[k, 1] = theirs[:, TILE : 2 * TILE]
        c_copy(k).start()

        soon = slot_of(n + 1)

        @pl.when((soon == 4) | ((soon >= 8) & (soon < 16)))
        def _():
            a_index_arrival(soon).wait_recv()

        @pl.when((soon == 4) | (soon == 8) | (soon == 9))
        def _():
            a_forward_index(soon).start()

        @pl.when((soon == 11) | (soon == 12))
        def _():
            a_forward_index_last(soon).start()

        @pl.when((soon >= 4) & (soon < 16))
        def _():
            make_table(soon)

        ours = terms(k, layer)
        own_ref[i, 0] = ours[:, 0:TILE]
        own_ref[i, 1] = ours[:, TILE : 2 * TILE]

        @pl.when(n < 15)
        def _():
            load_block(n + 1)

    for copy in (*a_first, *a_second):
        copy.wait_send()

    @pl.loop(2, 10)
    def _(k):
        a_forward_index(k).wait_send()
        a_forward(k).wait_send()

    a_forward_index_last(11).wait_send()
    a_forward_index_last(12).wait_send()
    a_forward_last().wait_send()
    a_forward_half(12).wait_send()
    a_forward_half(13).wait_send()
    for copy in (*b_own_up, *b_own_down, b_own_sib, *b_down_sib, *b_up_sib, *b_forward, *b_far_sib):
        copy.wait_send()

    @pl.loop(0, 16)
    def _(k):
        c_copy(k).wait()


def add_kernel(own_ref, arrived_ref, out_ref, total, sem):
    copies = []
    for n in range(4):
        part = pl.ds(4 * n, 4)
        total[part] = own_ref[part] + arrived_ref[part]
        copies.append(pltpu.make_async_copy(total.at[part], out_ref.at[part], sem.at[n]))
        copies[-1].start()
    for copy in copies:
        copy.wait()


def hbm(value):
    return pltpu.with_memory_space_constraint(value, pltpu.HBM)


def on_device(a_tiles, a_cols, b_tiles, b_rows, c_cols):
    f32, i32, bf16 = jnp.float32, jnp.int32, jnp.bfloat16
    dma = pltpu.SemaphoreType.DMA
    in_hbm = pl.BlockSpec(memory_space=pltpu.HBM)
    in_vmem = pl.BlockSpec(memory_space=pltpu.VMEM)
    part = jax.ShapeDtypeStruct((16, 2, TILE, TILE), f32)
    own, arrived = pl.pallas_call(
        kernel,
        out_shape=(part, part),
        in_specs=[in_hbm] * 5,
        out_specs=(in_vmem, in_vmem),
        scratch_shapes=[
            pltpu.VMEM((16, A_ROWS, TILE), f32),
            pltpu.VMEM((N_ROW, B_ROWS, TILE), f32),
            pltpu.VMEM((B_ALL + 1, TILE, TILE), bf16),
            pltpu.VMEM((B_ALL + 1, TILE, TILE), bf16),
            pltpu.SMEM((4, N_COL), i32),
            pltpu.SMEM((1, 1, SLOTS), i32),
            pltpu.SMEM((2, 1, SLOTS), i32),
            pltpu.VMEM((16, 8, TILE), i32),
            pltpu.VMEM((N_ROW, 8, TILE), i32),
            pltpu.VMEM((8, TILE), i32),
            pltpu.VMEM((16, 8, TILE), i32),
            pltpu.SMEM((16, 8, TILE), i32),
            pltpu.VMEM((2 * TILE, A_ROWS), bf16),
            pltpu.VMEM((2, A_ROWS, 2 * TILE), bf16),
            pltpu.VMEM((16, 2, TILE, TILE), f32),
            dma((6,)),
            dma((16,)),
            dma((17,)),
            dma((16,)),
            dma((N_ROW,)),
            dma((N_ROW,)),
            dma((17,)),
            dma((18,)),
            dma((25,)),
            dma((25,)),
            dma((16,)),
            dma((16,)),
            pltpu.SemaphoreType.REGULAR,
        ],
        compiler_params=pltpu.CompilerParams(
            collective_id=0, has_side_effects=True, vmem_limit_bytes=48 * 2**20
        ),
        cost_estimate=pl.CostEstimate(
            flops=6 * 16 * 28 * TILE**3, bytes_accessed=4 * 2**20, transcendentals=0
        ),
        name="gather_multiply_sum",
    )(
        hbm(c_cols.reshape(16, 4).T),
        hbm(a_cols),
        hbm(b_rows),
        hbm(a_tiles.reshape(A_ROWS, TILE)),
        hbm(b_tiles.reshape(B_ROWS, TILE)),
    )
    out = pl.pallas_call(
        add_kernel,
        out_shape=part,
        in_specs=[in_vmem, in_vmem],
        out_specs=in_hbm,
        scratch_shapes=[pltpu.VMEM((16, 2, TILE, TILE), f32), dma((4,))],
        compiler_params=pltpu.CompilerParams(vmem_limit_bytes=8 * 2**20),
        name="add_halves",
    )(own, arrived)
    return out[:, None]


def solution(mesh):
    return jax.shard_map(
        on_device,
        mesh=mesh,
        in_specs=(
            P(("row", "col"), "layer", None, None, None),
            P(("row", "col"), "layer", None),
            P(("row", "col"), "layer", None, None, None),
            P(("row", "col"), "layer", None),
            P("row", "col", None),
        ),
        out_specs=P("row", "col", "layer", None, None),
        check_vma=False,
    )
```

```python
import jax
import jax.numpy as jnp
from jax import lax
from jax.experimental import pallas as pl
from jax.experimental.pallas import tpu as pltpu
from jax.sharding import PartitionSpec as P

MESH = pl.DeviceIdType.MESH
TILE = 128
SLOTS = 7
A_ROWS = SLOTS * TILE
B_TILES = 2 * SLOTS
B_ROWS = B_TILES * TILE
N_ROW, N_COL = 8, 16
B_ALL = N_ROW * B_TILES
HALF_A = A_ROWS // 2
HALF_B = B_ROWS // 2


def source_col(k, z, x_hi):
    distance = (k + 2) // 4
    other = (k // 2 + 1 + (15 - k) // 15 + k // 15) % 2
    sign = 2 * (k % 2) - 1
    return ((z + sign * distance + 8) % 8) * 2 + (x_hi + other) % 2


def slot_of(n):
    m = n % 4
    third, fourth = (n // 8) * (1 - n // 12), n // 12
    return n + third * (2 - 4 * (m // 2)) + fourth * (2 - 3 * ((m + 3) // 4) + m // 3)


def kernel(
    want_ref,
    a_cols_ref,
    b_rows_ref,
    a_ref,
    b_ref,
    own_ref,
    arrived_ref,
    a_all,
    b_all,
    b_hi,
    b_lo,
    want,
    a_cols,
    b_rows,
    a_index_all,
    b_index_all,
    b_index_own,
    table_vmem,
    table,
    lhs,
    rhs,
    to_send,
    local_sem,
    table_sem,
    ai_send,
    ai_recv,
    bi_send,
    bi_recv,
    a_send,
    a_recv,
    b_send,
    b_recv,
    c_send,
    c_recv,
    answers,
):
    row, col, layer = lax.axis_index("row"), lax.axis_index("col"), lax.axis_index("layer")
    z, x_hi = col // 2, col % 2
    y, core = row // 2, row % 2

    def at(r, c, l):
        return (r, c, l)

    z_up = at(row, (col + 2) % N_COL, layer)
    z_down = at(row, (col + N_COL - 2) % N_COL, layer)
    x_far = at(row, z * 2 + (x_hi + 1) % 2, layer)
    y_up_row, y_down_row, y_far_row = (row + 2) % N_ROW, (row + 6) % N_ROW, (row + 4) % N_ROW
    y_up, y_down = at(y_up_row, col, layer), at(y_down_row, col, layer)
    sibling_row = y * 2 + (core + 1) % 2
    sibling = at(sibling_row, col, layer)
    sib_up, sib_down, sib_far = (
        (sibling_row + 2) % N_ROW,
        (sibling_row + 6) % N_ROW,
        (sibling_row + 4) % N_ROW,
    )
    partner = at(row, col, 1 - layer)

    def remote(src, dst, send_sem, recv_sem, device):
        return pltpu.make_async_remote_copy(
            src_ref=src,
            dst_ref=dst,
            send_sem=send_sem,
            recv_sem=recv_sem,
            device_id=device,
            device_id_type=MESH,
        )

    a_local = pltpu.make_async_copy(a_ref, a_all.at[0], local_sem.at[0])
    b_local = pltpu.make_async_copy(b_ref, b_all.at[row], local_sem.at[1])
    scalars = [
        pltpu.make_async_copy(src, dst, local_sem.at[3 + n])
        for n, (src, dst) in enumerate(
            ((a_cols_ref, a_cols), (b_rows_ref, b_rows), (want_ref, want))
        )
    ]

    other = (core + 1) % 2
    pairs = (
        (z_up, (z < 4) | (z == 5)),
        (z_down, (z == 0) | (z == 5) | (z == 7)),
        (x_far, x_hi == 0),
        (partner, layer == 0),
        (at(y_far_row, col, layer), y < 2),
        (at((y + 2) % 4 * 2 + other, col, layer), y < 2),
        (at((y + 1) % 4 * 2 + other, col, layer), y < 3),
        (at((y + 3) % 4 * 2 + other, col, layer), y == 0),
    )
    is_0, is_4, is_5, is_6 = (
        (z + 8 - v) // 8 * (1 - (z + 7 - v) // 8) for v in (0, 4, 5, 6)
    )
    before = 1 - is_0 + is_4 - is_5 + is_6 + x_hi + layer + 2 * (y // 2) + (y + 1) // 2
    after = len(pairs) - before
    barrier = pltpu.get_barrier_semaphore()
    for device in (y_up, y_down, sibling):
        pl.semaphore_signal(barrier, inc=1, device_id=device, device_id_type=MESH)
    for device, first in pairs:

        @pl.when(first)
        def _():
            pl.semaphore_signal(barrier, inc=1, device_id=device, device_id_type=MESH)

    for copy in scalars:
        copy.start()
    b_local.start()
    a_local.start()
    pl.semaphore_wait(barrier, 3 + before)

    halves = (pl.ds(0, HALF_B), pl.ds(HALF_B, HALF_B))

    def b_copy(r, part, n, device):
        return remote(b_all.at[r, part], b_all.at[r, part], b_send.at[n], b_recv.at[n], device)

    def b_own(half, n, device):
        part = halves[half]
        return remote(b_ref.at[part], b_all.at[row, part], b_send.at[n], b_recv.at[n], device)

    b_own_up = [b_own(0, 0, y_up), b_own(1, 1, y_up)]
    b_own_down = [b_own(1, 2, y_down), b_own(0, 3, y_down)]
    b_own_sib = remote(b_ref, b_all.at[row], b_send.at[4], b_recv.at[4], sibling)
    b_down_sib = [b_copy(y_down_row, halves[half], 5 + half, sibling) for half in (0, 1)]
    b_up_sib = [b_copy(y_up_row, halves[half], 8 - half, sibling) for half in (1, 0)]
    b_pieces = ((0, 3), (7, 3), (3, 2), (10, 2), (5, 1), (12, 1), (6, 1), (13, 1))
    b_forward, b_far_sib = [], []
    for n, (tile, count) in enumerate(b_pieces):
        part = pl.ds(tile * TILE, count * TILE)
        came, goes = (y_down_row, y_up) if n % 2 == 0 else (y_up_row, y_down)
        b_forward.append(b_copy(came, part, 9 + n, goes))
        b_far_sib.append(b_copy(y_far_row, part, 17 + n, sibling))
    for n in range(2):
        b_own_up[n].start()
        b_own_down[n].start()
    b_own_sib.start()
    for device, first in pairs:

        @pl.when(jnp.logical_not(first))
        def _():
            pl.semaphore_signal(answers, inc=1, device_id=device, device_id_type=MESH)


    def b_index_copy(d):
        return remote(
            b_index_own,
            b_index_all.at[row],
            bi_send.at[d],
            bi_recv.at[d],
            at((row + d) % N_ROW, col, layer),
        )

    for copy in scalars:
        copy.wait()
    lane = lax.broadcasted_iota(jnp.int32, (8, TILE), 1)
    sublane = lax.broadcasted_iota(jnp.int32, (8, TILE), 0)
    a_index = jnp.full((8, TILE), -1, jnp.int32)
    for s in range(SLOTS):
        a_index = jnp.where(sublane == s, a_cols[0, 0, s], a_index)
    b_index = jnp.full((8, TILE), -5, jnp.int32)
    for t in range(B_TILES):
        b_index = jnp.where(lane == row * B_TILES + t, b_rows[t // SLOTS, 0, t % SLOTS], b_index)
    b_index_own[...] = b_index
    b_index_all[row] = b_index
    a_index_all[0] = a_index

    class Both:
        def __init__(self, *copies):
            self.copies = copies

        def start(self):
            for copy in self.copies:
                copy.start()

        def wait_send(self):
            for copy in self.copies:
                copy.wait_send()

    def a_index_copy(src, dst, n, device):
        return remote(
            a_index_all.at[src], a_index_all.at[dst], ai_send.at[n], ai_recv.at[dst], device
        )

    def a_copy(src, dst, n, device):
        block = a_ref if src == 0 else a_all.at[src]
        return Both(
            a_index_copy(src, dst, n, device),
            remote(block, a_all.at[dst], a_send.at[n], a_recv.at[dst], device),
        )

    a_first = [
        a_copy(0, 2, 14, z_up),
        a_copy(0, 3, 15, z_down),
        a_copy(0, 1, 16, x_far),
    ]
    a_second = [a_copy(1, 4, 0, z_up), a_copy(3, 5, 1, x_far)]

    @pl.when(after > 0)
    def _():
        pl.semaphore_wait(answers, after)

    for copy in a_first:
        copy.start()

    @pl.loop(1, N_ROW)
    def _(d):
        b_index_copy(d).start()

    b_hi[B_ALL] = jnp.zeros((TILE, TILE), jnp.bfloat16)
    b_lo[B_ALL] = jnp.zeros((TILE, TILE), jnp.bfloat16)

    def split_b(r, first=0, count=B_TILES):
        @pl.loop(first, first + count)
        def _(t):
            value = b_all[r, pl.ds(pl.multiple_of(t * TILE, TILE), TILE), :]
            hi = value.astype(jnp.bfloat16)
            b_hi[r * B_TILES + t] = hi
            b_lo[r * B_TILES + t] = (value - hi.astype(jnp.float32)).astype(jnp.bfloat16)

    def ahead(k):
        return at(row, (col + (1 - k % 2) * 2 + (k % 2) * (N_COL - 2)) % N_COL, layer)

    def a_forward_index(k):
        return a_index_copy(k, k + 4, k, ahead(k))

    def a_forward_index_last(k):
        return a_index_copy(k, 14 + (k - 10) // 2, k, ahead(k))

    def a_forward(k):
        return remote(a_all.at[k], a_all.at[k + 4], a_send.at[k], a_recv.at[k + 4], ahead(k))

    def a_forward_last():
        return remote(a_all.at[11], a_all.at[14], a_send.at[11], a_recv.at[14], ahead(11))

    def a_forward_half(k):
        part = pl.ds(pl.multiple_of((k % 2) * HALF_A, HALF_A), HALF_A)
        return remote(
            a_all.at[k, part], a_all.at[15, part], a_send.at[k], a_recv.at[k + 3], ahead(k)
        )

    def a_index_arrival(k):
        return remote(a_index_all.at[k], a_index_all.at[k], ai_send.at[k], ai_recv.at[k], z_up)

    def a_arrival(k):
        return remote(a_all.at[k], a_all.at[k], a_send.at[k], a_recv.at[k], z_up)

    def a_arrival_half(n):
        part = pl.ds(n * HALF_A, HALF_A)
        return remote(
            a_all.at[15, part], a_all.at[15, part], a_send.at[15], a_recv.at[15 + n], z_up
        )

    def load_block(n):
        k = slot_of(n)

        @pl.when(n == 2)
        def _():
            a_arrival(4).wait_recv()
            a_forward(4).start()

        @pl.when(n == 10)
        def _():
            for j in (9, 8):
                a_arrival(j).wait_recv()
                a_forward(j).start()

        @pl.when(n == 6)
        def _():
            a_arrival(11).wait_recv()
            a_forward_last().start()

        @pl.when(n == 8)
        def _():
            a_arrival(10).wait_recv()

        @pl.when(k == 14)
        def _():
            a_arrival(14).wait_recv()

        @pl.when(k == 12)
        def _():
            for j in (13, 12):
                a_arrival(j).wait_recv()
                a_forward_half(j).start()

        @pl.when(k == 15)
        def _():
            a_arrival_half(0).wait_recv()
            a_arrival_half(1).wait_recv()

        for s in range(SLOTS):
            value = a_all[k, s * TILE : (s + 1) * TILE, :]
            hi = value.astype(jnp.bfloat16)
            lhs[0:TILE, s * TILE : (s + 1) * TILE] = hi
            lhs[TILE : 2 * TILE, s * TILE : (s + 1) * TILE] = (
                value - hi.astype(jnp.float32)
            ).astype(jnp.bfloat16)

    def table_copy(k):
        return pltpu.make_async_copy(table_vmem.at[k], table.at[k], table_sem.at[k])

    def make_table(k):
        b_index = b_index_all[0]
        for r in range(1, N_ROW):
            b_index = jnp.maximum(b_index, b_index_all[r])
        i = source_col(k, z, x_hi)
        a_index = a_index_all[k]
        found = jnp.full((8, TILE), B_ALL, jnp.int32)
        for q in range(4):
            wanted = want[q, i]
            wanted_panel = wanted // 32 * 2 + wanted % 2
            match = (a_index == b_index) & (lane // SLOTS == wanted_panel)
            position = jnp.min(jnp.where(match, lane, B_ALL), axis=1, keepdims=True)
            found = jnp.where(lane == q, position, found)
        table_vmem[k] = found
        table_copy(k).start()

    b_local.wait()
    split_b(row)
    b_own_sib.wait_recv()
    split_b(sibling_row)
    for k in (3, 2):
        a_index_arrival(k).wait_recv()
        a_forward_index(k).start()
        a_arrival(k).wait_recv()
        a_forward(k).start()
        if k == 3:
            a_second[1].start()
    b_own_up[0].wait_recv()
    for copy in b_forward[0::2]:
        copy.start()
    b_own_down[0].wait_recv()
    for copy in b_forward[1::2]:
        copy.start()
    a_index_arrival(1).wait_recv()
    a_arrival(1).wait_recv()
    a_second[0].start()
    b_down_sib[0].start()
    b_up_sib[0].start()
    b_own_up[1].wait_recv()
    b_down_sib[1].start()
    b_own_down[1].wait_recv()
    b_up_sib[1].start()
    split_b(y_down_row)
    split_b(y_up_row)

    @pl.loop(6, 8)
    def _(k):
        a_index_arrival(k).wait_recv()
        a_forward_index(k).start()
        a_arrival(k).wait_recv()
        a_forward(k).start()

    b_down_sib[0].wait_recv()
    b_down_sib[1].wait_recv()
    split_b(sib_down)
    b_up_sib[0].wait_recv()
    b_up_sib[1].wait_recv()
    split_b(sib_up)

    @pl.loop(1, N_ROW)
    def _(d):
        b_index_copy(d).wait()

    @pl.loop(0, 4)
    def _(k):
        make_table(k)

    a_index_arrival(5).wait_recv()
    a_forward_index(5).start()
    a_arrival(5).wait_recv()
    a_forward(5).start()
    a_local.wait()
    load_block(0)
    for n in range(len(b_pieces)):
        b_forward[n].wait_recv()
        b_far_sib[n].start()

    for tile, count in b_pieces:
        split_b(y_far_row, tile, count)
    for n, (tile, count) in enumerate(b_pieces):
        b_far_sib[n].wait_recv()
        split_b(sib_far, tile, count)

    def c_copy(k):
        return remote(
            to_send.at[k],
            arrived_ref.at[source_col(k, z, x_hi)],
            c_send.at[k],
            c_recv.at[k],
            partner,
        )

    def terms(k, half):
        for s in range(SLOTS):
            for n in range(2):
                t = table[k, s, half * 2 + n]
                rhs[0, s * TILE : (s + 1) * TILE, n * TILE : (n + 1) * TILE] = b_hi[t]
                rhs[1, s * TILE : (s + 1) * TILE, n * TILE : (n + 1) * TILE] = b_lo[t]
        both = jnp.dot(lhs[...], rhs[0], preferred_element_type=jnp.float32)
        low = jnp.dot(lhs[0:TILE, :], rhs[1], preferred_element_type=jnp.float32)
        return both[0:TILE] + (both[TILE : 2 * TILE] + low)

    @pl.loop(0, 16)
    def _(n):
        k = slot_of(n)
        i = source_col(k, z, x_hi)
        table_copy(k).wait()
        theirs = terms(k, 1 - layer)
        to_send[k, 0] = theirs[:, 0:TILE]
        to_send[k, 1] = theirs[:, TILE : 2 * TILE]
        c_copy(k).start()

        soon = slot_of(n + 1)

        @pl.when((soon == 4) | ((soon >= 8) & (soon < 16)))
        def _():
            a_index_arrival(soon).wait_recv()

        @pl.when((soon == 4) | (soon == 8) | (soon == 9))
        def _():
            a_forward_index(soon).start()

        @pl.when((soon == 11) | (soon == 12))
        def _():
            a_forward_index_last(soon).start()

        @pl.when((soon >= 4) & (soon < 16))
        def _():
            make_table(soon)

        ours = terms(k, layer)
        own_ref[i, 0] = ours[:, 0:TILE]
        own_ref[i, 1] = ours[:, TILE : 2 * TILE]

        @pl.when(n < 15)
        def _():
            load_block(n + 1)

    for copy in (*a_first, *a_second):
        copy.wait_send()

    @pl.loop(2, 10)
    def _(k):
        a_forward_index(k).wait_send()
        a_forward(k).wait_send()

    a_forward_index_last(11).wait_send()
    a_forward_index_last(12).wait_send()
    a_forward_last().wait_send()
    a_forward_half(12).wait_send()
    a_forward_half(13).wait_send()
    for copy in (*b_own_up, *b_own_down, b_own_sib, *b_down_sib, *b_up_sib, *b_forward, *b_far_sib):
        copy.wait_send()

    @pl.loop(0, 16)
    def _(k):
        c_copy(k).wait()


def add_kernel(own_ref, arrived_ref, out_ref, total, sem):
    copies = []
    for n in range(4):
        part = pl.ds(4 * n, 4)
        total[part] = own_ref[part] + arrived_ref[part]
        copies.append(pltpu.make_async_copy(total.at[part], out_ref.at[part], sem.at[n]))
        copies[-1].start()
    for copy in copies:
        copy.wait()


def hbm(value):
    return pltpu.with_memory_space_constraint(value, pltpu.HBM)


def on_device(a_tiles, a_cols, b_tiles, b_rows, c_cols):
    f32, i32, bf16 = jnp.float32, jnp.int32, jnp.bfloat16
    dma = pltpu.SemaphoreType.DMA
    in_hbm = pl.BlockSpec(memory_space=pltpu.HBM)
    in_vmem = pl.BlockSpec(memory_space=pltpu.VMEM)
    part = jax.ShapeDtypeStruct((16, 2, TILE, TILE), f32)
    own, arrived = pl.pallas_call(
        kernel,
        out_shape=(part, part),
        in_specs=[in_hbm] * 5,
        out_specs=(in_vmem, in_vmem),
        scratch_shapes=[
            pltpu.VMEM((16, A_ROWS, TILE), f32),
            pltpu.VMEM((N_ROW, B_ROWS, TILE), f32),
            pltpu.VMEM((B_ALL + 1, TILE, TILE), bf16),
            pltpu.VMEM((B_ALL + 1, TILE, TILE), bf16),
            pltpu.SMEM((4, N_COL), i32),
            pltpu.SMEM((1, 1, SLOTS), i32),
            pltpu.SMEM((2, 1, SLOTS), i32),
            pltpu.VMEM((16, 8, TILE), i32),
            pltpu.VMEM((N_ROW, 8, TILE), i32),
            pltpu.VMEM((8, TILE), i32),
            pltpu.VMEM((16, 8, TILE), i32),
            pltpu.SMEM((16, 8, TILE), i32),
            pltpu.VMEM((2 * TILE, A_ROWS), bf16),
            pltpu.VMEM((2, A_ROWS, 2 * TILE), bf16),
            pltpu.VMEM((16, 2, TILE, TILE), f32),
            dma((6,)),
            dma((16,)),
            dma((17,)),
            dma((16,)),
            dma((N_ROW,)),
            dma((N_ROW,)),
            dma((17,)),
            dma((18,)),
            dma((25,)),
            dma((25,)),
            dma((16,)),
            dma((16,)),
            pltpu.SemaphoreType.REGULAR,
        ],
        compiler_params=pltpu.CompilerParams(
            collective_id=0, has_side_effects=True, vmem_limit_bytes=48 * 2**20
        ),
        cost_estimate=pl.CostEstimate(
            flops=6 * 16 * 28 * TILE**3, bytes_accessed=4 * 2**20, transcendentals=0
        ),
        name="gather_multiply_sum",
    )(
        hbm(c_cols.reshape(16, 4).T),
        hbm(a_cols),
        hbm(b_rows),
        hbm(a_tiles.reshape(A_ROWS, TILE)),
        hbm(b_tiles.reshape(B_ROWS, TILE)),
    )
    out = pl.pallas_call(
        add_kernel,
        out_shape=part,
        in_specs=[in_vmem, in_vmem],
        out_specs=in_hbm,
        scratch_shapes=[pltpu.VMEM((16, 2, TILE, TILE), f32), dma((4,))],
        compiler_params=pltpu.CompilerParams(vmem_limit_bytes=8 * 2**20),
        name="add_halves",
    )(own, arrived)
    return out[:, None]


def solution(mesh):
    return jax.shard_map(
        on_device,
        mesh=mesh,
        in_specs=(
            P(("row", "col"), "layer", None, None, None),
            P(("row", "col"), "layer", None),
            P(("row", "col"), "layer", None, None, None),
            P(("row", "col"), "layer", None),
            P("row", "col", None),
        ),
        out_specs=P("row", "col", "layer", None, None),
        check_vma=False,
    )
```

```python
import jax
import jax.numpy as jnp
from jax import lax
from jax.experimental import pallas as pl
from jax.experimental.pallas import tpu as pltpu
from jax.sharding import PartitionSpec as P

MESH = pl.DeviceIdType.MESH
TILE = 128
SLOTS = 7
A_ROWS = SLOTS * TILE
B_TILES = 2 * SLOTS
B_ROWS = B_TILES * TILE
N_ROW, N_COL = 8, 16
B_ALL = N_ROW * B_TILES
HALF_A = A_ROWS // 2
HALF_B = B_ROWS // 2


def source_col(k, z, x_hi):
    distance = (k + 2) // 4
    other = (k // 2 + 1 + (15 - k) // 15 + k // 15) % 2
    sign = 2 * (k % 2) - 1
    return ((z + sign * distance + 8) % 8) * 2 + (x_hi + other) % 2


def slot_of(n):
    m = n % 4
    third, fourth = (n // 8) * (1 - n // 12), n // 12
    return n + third * (2 - 4 * (m // 2)) + fourth * (2 - 3 * ((m + 3) // 4) + m // 3)


def kernel(
    want_ref,
    a_cols_ref,
    b_rows_ref,
    a_ref,
    b_ref,
    own_ref,
    arrived_ref,
    a_all,
    b_all,
    b_hi,
    b_lo,
    want,
    a_cols,
    b_rows,
    a_index_all,
    b_index_all,
    b_index_own,
    table_vmem,
    table,
    lhs,
    rhs,
    to_send,
    local_sem,
    table_sem,
    ai_send,
    ai_recv,
    bi_send,
    bi_recv,
    a_send,
    a_recv,
    b_send,
    b_recv,
    c_send,
    c_recv,
    answers,
):
    row, col, layer = lax.axis_index("row"), lax.axis_index("col"), lax.axis_index("layer")
    z, x_hi = col // 2, col % 2
    y, core = row // 2, row % 2

    def at(r, c, l):
        return (r, c, l)

    z_up = at(row, (col + 2) % N_COL, layer)
    z_down = at(row, (col + N_COL - 2) % N_COL, layer)
    x_far = at(row, z * 2 + (x_hi + 1) % 2, layer)
    y_up_row, y_down_row, y_far_row = (row + 2) % N_ROW, (row + 6) % N_ROW, (row + 4) % N_ROW
    y_up, y_down = at(y_up_row, col, layer), at(y_down_row, col, layer)
    sibling_row = y * 2 + (core + 1) % 2
    sibling = at(sibling_row, col, layer)
    sib_up, sib_down, sib_far = (
        (sibling_row + 2) % N_ROW,
        (sibling_row + 6) % N_ROW,
        (sibling_row + 4) % N_ROW,
    )
    partner = at(row, col, 1 - layer)

    def remote(src, dst, send_sem, recv_sem, device):
        return pltpu.make_async_remote_copy(
            src_ref=src,
            dst_ref=dst,
            send_sem=send_sem,
            recv_sem=recv_sem,
            device_id=device,
            device_id_type=MESH,
        )

    a_local = pltpu.make_async_copy(a_ref, a_all.at[0], local_sem.at[0])
    b_local = pltpu.make_async_copy(b_ref, b_all.at[row], local_sem.at[1])
    scalars = [
        pltpu.make_async_copy(src, dst, local_sem.at[3 + n])
        for n, (src, dst) in enumerate(
            ((a_cols_ref, a_cols), (b_rows_ref, b_rows), (want_ref, want))
        )
    ]

    other = (core + 1) % 2
    pairs = (
        (z_up, (z < 4) | (z == 5)),
        (z_down, (z == 0) | (z == 5) | (z == 7)),
        (x_far, x_hi == 0),
        (partner, layer == 0),
        (at(y_far_row, col, layer), y < 2),
        (at((y + 2) % 4 * 2 + other, col, layer), y < 2),
        (at((y + 1) % 4 * 2 + other, col, layer), y < 3),
        (at((y + 3) % 4 * 2 + other, col, layer), y == 0),
    )
    is_0, is_4, is_5, is_6 = (
        (z + 8 - v) // 8 * (1 - (z + 7 - v) // 8) for v in (0, 4, 5, 6)
    )
    before = 1 - is_0 + is_4 - is_5 + is_6 + x_hi + layer + 2 * (y // 2) + (y + 1) // 2
    after = len(pairs) - before
    barrier = pltpu.get_barrier_semaphore()
    for device in (y_up, y_down, sibling):
        pl.semaphore_signal(barrier, inc=1, device_id=device, device_id_type=MESH)
    for device, first in pairs:

        @pl.when(first)
        def _():
            pl.semaphore_signal(barrier, inc=1, device_id=device, device_id_type=MESH)

    for copy in scalars:
        copy.start()
    b_local.start()
    a_local.start()
    pl.semaphore_wait(barrier, 3 + before)

    halves = (pl.ds(0, HALF_B), pl.ds(HALF_B, HALF_B))

    def b_copy(r, part, n, device):
        return remote(b_all.at[r, part], b_all.at[r, part], b_send.at[n], b_recv.at[n], device)

    def b_own(half, n, device):
        part = halves[half]
        return remote(b_ref.at[part], b_all.at[row, part], b_send.at[n], b_recv.at[n], device)

    b_own_up = [b_own(0, 0, y_up), b_own(1, 1, y_up)]
    b_own_down = [b_own(1, 2, y_down), b_own(0, 3, y_down)]
    b_own_sib = remote(b_ref, b_all.at[row], b_send.at[4], b_recv.at[4], sibling)
    b_down_sib = [b_copy(y_down_row, halves[half], 5 + half, sibling) for half in (0, 1)]
    b_up_sib = [b_copy(y_up_row, halves[half], 8 - half, sibling) for half in (1, 0)]
    b_pieces = ((0, 3), (7, 3), (3, 2), (10, 2), (5, 1), (12, 1), (6, 1), (13, 1))
    b_forward, b_far_sib = [], []
    for n, (tile, count) in enumerate(b_pieces):
        part = pl.ds(tile * TILE, count * TILE)
        came, goes = (y_down_row, y_up) if n % 2 == 0 else (y_up_row, y_down)
        b_forward.append(b_copy(came, part, 9 + n, goes))
        b_far_sib.append(b_copy(y_far_row, part, 17 + n, sibling))
    for n in range(2):
        b_own_up[n].start()
        b_own_down[n].start()
    b_own_sib.start()
    for device, first in pairs:

        @pl.when(jnp.logical_not(first))
        def _():
            pl.semaphore_signal(answers, inc=1, device_id=device, device_id_type=MESH)


    def b_index_copy(d):
        return remote(
            b_index_own,
            b_index_all.at[row],
            bi_send.at[d],
            bi_recv.at[d],
            at((row + d) % N_ROW, col, layer),
        )

    for copy in scalars:
        copy.wait()
    lane = lax.broadcasted_iota(jnp.int32, (8, TILE), 1)
    sublane = lax.broadcasted_iota(jnp.int32, (8, TILE), 0)
    a_index = jnp.full((8, TILE), -1, jnp.int32)
    for s in range(SLOTS):
        a_index = jnp.where(sublane == s, a_cols[0, 0, s], a_index)
    b_index = jnp.full((8, TILE), -5, jnp.int32)
    for t in range(B_TILES):
        b_index = jnp.where(lane == row * B_TILES + t, b_rows[t // SLOTS, 0, t % SLOTS], b_index)
    b_index_own[...] = b_index
    b_index_all[row] = b_index
    a_index_all[0] = a_index

    class Both:
        def __init__(self, *copies):
            self.copies = copies

        def start(self):
            for copy in self.copies:
                copy.start()

        def wait_send(self):
            for copy in self.copies:
                copy.wait_send()

    def a_index_copy(src, dst, n, device):
        return remote(
            a_index_all.at[src], a_index_all.at[dst], ai_send.at[n], ai_recv.at[dst], device
        )

    def a_copy(src, dst, n, device):
        block = a_ref if src == 0 else a_all.at[src]
        return Both(
            a_index_copy(src, dst, n, device),
            remote(block, a_all.at[dst], a_send.at[n], a_recv.at[dst], device),
        )

    a_first = [
        a_copy(0, 2, 14, z_up),
        a_copy(0, 3, 15, z_down),
        a_copy(0, 1, 16, x_far),
    ]
    a_second = [a_copy(1, 4, 0, z_up), a_copy(3, 5, 1, x_far)]

    @pl.when(after > 0)
    def _():
        pl.semaphore_wait(answers, after)

    for copy in a_first:
        copy.start()

    @pl.loop(1, N_ROW)
    def _(d):
        b_index_copy(d).start()

    b_hi[B_ALL] = jnp.zeros((TILE, TILE), jnp.bfloat16)
    b_lo[B_ALL] = jnp.zeros((TILE, TILE), jnp.bfloat16)

    def split_b(r, first=0, count=B_TILES):
        @pl.loop(first, first + count)
        def _(t):
            value = b_all[r, pl.ds(pl.multiple_of(t * TILE, TILE), TILE), :]
            hi = value.astype(jnp.bfloat16)
            b_hi[r * B_TILES + t] = hi
            b_lo[r * B_TILES + t] = (value - hi.astype(jnp.float32)).astype(jnp.bfloat16)

    def ahead(k):
        return at(row, (col + (1 - k % 2) * 2 + (k % 2) * (N_COL - 2)) % N_COL, layer)

    def a_forward_index(k):
        return a_index_copy(k, k + 4, k, ahead(k))

    def a_forward_index_last(k):
        return a_index_copy(k, 14 + (k - 10) // 2, k, ahead(k))

    def a_forward(k):
        return remote(a_all.at[k], a_all.at[k + 4], a_send.at[k], a_recv.at[k + 4], ahead(k))

    def a_forward_last():
        return remote(a_all.at[11], a_all.at[14], a_send.at[11], a_recv.at[14], ahead(11))

    def a_forward_half(k):
        part = pl.ds(pl.multiple_of((k % 2) * HALF_A, HALF_A), HALF_A)
        return remote(
            a_all.at[k, part], a_all.at[15, part], a_send.at[k], a_recv.at[k + 3], ahead(k)
        )

    def a_index_arrival(k):
        return remote(a_index_all.at[k], a_index_all.at[k], ai_send.at[k], ai_recv.at[k], z_up)

    def a_arrival(k):
        return remote(a_all.at[k], a_all.at[k], a_send.at[k], a_recv.at[k], z_up)

    def a_arrival_half(n):
        part = pl.ds(n * HALF_A, HALF_A)
        return remote(
            a_all.at[15, part], a_all.at[15, part], a_send.at[15], a_recv.at[15 + n], z_up
        )

    def load_block(n):
        k = slot_of(n)

        @pl.when(n == 2)
        def _():
            a_arrival(4).wait_recv()
            a_forward(4).start()

        @pl.when(n == 10)
        def _():
            for j in (9, 8):
                a_arrival(j).wait_recv()
                a_forward(j).start()

        @pl.when(n == 6)
        def _():
            a_arrival(11).wait_recv()
            a_forward_last().start()

        @pl.when(n == 8)
        def _():
            a_arrival(10).wait_recv()

        @pl.when(k == 14)
        def _():
            a_arrival(14).wait_recv()

        @pl.when(k == 12)
        def _():
            for j in (13, 12):
                a_arrival(j).wait_recv()
                a_forward_half(j).start()

        @pl.when(k == 15)
        def _():
            a_arrival_half(0).wait_recv()
            a_arrival_half(1).wait_recv()

        for s in range(SLOTS):
            value = a_all[k, s * TILE : (s + 1) * TILE, :]
            hi = value.astype(jnp.bfloat16)
            lhs[0:TILE, s * TILE : (s + 1) * TILE] = hi
            lhs[TILE : 2 * TILE, s * TILE : (s + 1) * TILE] = (
                value - hi.astype(jnp.float32)
            ).astype(jnp.bfloat16)

    def table_copy(k):
        return pltpu.make_async_copy(table_vmem.at[k], table.at[k], table_sem.at[k])

    def make_table(k):
        b_index = b_index_all[0]
        for r in range(1, N_ROW):
            b_index = jnp.maximum(b_index, b_index_all[r])
        i = source_col(k, z, x_hi)
        a_index = a_index_all[k]
        found = jnp.full((8, TILE), B_ALL, jnp.int32)
        for q in range(4):
            wanted = want[q, i]
            wanted_panel = wanted // 32 * 2 + wanted % 2
            match = (a_index == b_index) & (lane // SLOTS == wanted_panel)
            position = jnp.min(jnp.where(match, lane, B_ALL), axis=1, keepdims=True)
            found = jnp.where(lane == q, position, found)
        table_vmem[k] = found
        table_copy(k).start()

    b_local.wait()
    split_b(row)
    b_own_sib.wait_recv()
    split_b(sibling_row)
    for k in (3, 2):
        a_index_arrival(k).wait_recv()
        a_forward_index(k).start()
        a_arrival(k).wait_recv()
        a_forward(k).start()
        if k == 3:
            a_second[1].start()
    b_own_up[0].wait_recv()
    for copy in b_forward[0::2]:
        copy.start()
    b_own_down[0].wait_recv()
    for copy in b_forward[1::2]:
        copy.start()
    a_index_arrival(1).wait_recv()
    a_arrival(1).wait_recv()
    a_second[0].start()
    b_down_sib[0].start()
    b_up_sib[0].start()
    b_own_up[1].wait_recv()
    b_down_sib[1].start()
    b_own_down[1].wait_recv()
    b_up_sib[1].start()
    split_b(y_down_row)
    split_b(y_up_row)

    @pl.loop(6, 8)
    def _(k):
        a_index_arrival(k).wait_recv()
        a_forward_index(k).start()
        a_arrival(k).wait_recv()
        a_forward(k).start()

    b_down_sib[0].wait_recv()
    b_down_sib[1].wait_recv()
    split_b(sib_down)
    b_up_sib[0].wait_recv()
    b_up_sib[1].wait_recv()
    split_b(sib_up)

    @pl.loop(1, N_ROW)
    def _(d):
        b_index_copy(d).wait()

    @pl.loop(0, 4)
    def _(k):
        make_table(k)

    a_index_arrival(5).wait_recv()
    a_forward_index(5).start()
    a_arrival(5).wait_recv()
    a_forward(5).start()
    a_local.wait()
    load_block(0)
    for n in range(len(b_pieces)):
        b_forward[n].wait_recv()
        b_far_sib[n].start()

    for tile, count in b_pieces:
        split_b(y_far_row, tile, count)
    for n, (tile, count) in enumerate(b_pieces):
        b_far_sib[n].wait_recv()
        split_b(sib_far, tile, count)

    def c_copy(k, n):
        return remote(
            to_send.at[k, n],
            arrived_ref.at[source_col(k, z, x_hi), n],
            c_send.at[k, n],
            c_recv.at[k, n],
            partner,
        )

    def gather(k, half, n):
        for s in range(SLOTS):
            t = table[k, s, half * 2 + n]
            rhs[0, s * TILE : (s + 1) * TILE, n * TILE : (n + 1) * TILE] = b_hi[t]
            rhs[1, s * TILE : (s + 1) * TILE, n * TILE : (n + 1) * TILE] = b_lo[t]

    def product(columns):
        both = jnp.dot(lhs[...], rhs[0, :, columns], preferred_element_type=jnp.float32)
        low = jnp.dot(lhs[0:TILE, :], rhs[1, :, columns], preferred_element_type=jnp.float32)
        return both[0:TILE] + (both[TILE : 2 * TILE] + low)

    @pl.loop(0, 16)
    def _(n):
        k = slot_of(n)
        i = source_col(k, z, x_hi)
        table_copy(k).wait()
        for m in range(2):
            gather(k, 1 - layer, m)
            to_send[k, m] = product(slice(m * TILE, (m + 1) * TILE))
            c_copy(k, m).start()

        soon = slot_of(n + 1)

        @pl.when((soon == 4) | ((soon >= 8) & (soon < 16)))
        def _():
            a_index_arrival(soon).wait_recv()

        @pl.when((soon == 4) | (soon == 8) | (soon == 9))
        def _():
            a_forward_index(soon).start()

        @pl.when((soon == 11) | (soon == 12))
        def _():
            a_forward_index_last(soon).start()

        @pl.when((soon >= 4) & (soon < 16))
        def _():
            make_table(soon)

        gather(k, layer, 0)
        gather(k, layer, 1)
        ours = product(slice(0, 2 * TILE))
        own_ref[i, 0] = ours[:, 0:TILE]
        own_ref[i, 1] = ours[:, TILE : 2 * TILE]

        @pl.when(n < 15)
        def _():
            load_block(n + 1)

    for copy in (*a_first, *a_second):
        copy.wait_send()

    @pl.loop(2, 10)
    def _(k):
        a_forward_index(k).wait_send()
        a_forward(k).wait_send()

    a_forward_index_last(11).wait_send()
    a_forward_index_last(12).wait_send()
    a_forward_last().wait_send()
    a_forward_half(12).wait_send()
    a_forward_half(13).wait_send()
    for copy in (*b_own_up, *b_own_down, b_own_sib, *b_down_sib, *b_up_sib, *b_forward, *b_far_sib):
        copy.wait_send()

    @pl.loop(0, 16)
    def _(k):
        c_copy(k, 0).wait()
        c_copy(k, 1).wait()


def add_kernel(own_ref, arrived_ref, out_ref, total, sem):
    copies = []
    for n in range(4):
        part = pl.ds(4 * n, 4)
        total[part] = own_ref[part] + arrived_ref[part]
        copies.append(pltpu.make_async_copy(total.at[part], out_ref.at[part], sem.at[n]))
        copies[-1].start()
    for copy in copies:
        copy.wait()


def hbm(value):
    return pltpu.with_memory_space_constraint(value, pltpu.HBM)


def on_device(a_tiles, a_cols, b_tiles, b_rows, c_cols):
    f32, i32, bf16 = jnp.float32, jnp.int32, jnp.bfloat16
    dma = pltpu.SemaphoreType.DMA
    in_hbm = pl.BlockSpec(memory_space=pltpu.HBM)
    in_vmem = pl.BlockSpec(memory_space=pltpu.VMEM)
    part = jax.ShapeDtypeStruct((16, 2, TILE, TILE), f32)
    own, arrived = pl.pallas_call(
        kernel,
        out_shape=(part, part),
        in_specs=[in_hbm] * 5,
        out_specs=(in_vmem, in_vmem),
        scratch_shapes=[
            pltpu.VMEM((16, A_ROWS, TILE), f32),
            pltpu.VMEM((N_ROW, B_ROWS, TILE), f32),
            pltpu.VMEM((B_ALL + 1, TILE, TILE), bf16),
            pltpu.VMEM((B_ALL + 1, TILE, TILE), bf16),
            pltpu.SMEM((4, N_COL), i32),
            pltpu.SMEM((1, 1, SLOTS), i32),
            pltpu.SMEM((2, 1, SLOTS), i32),
            pltpu.VMEM((16, 8, TILE), i32),
            pltpu.VMEM((N_ROW, 8, TILE), i32),
            pltpu.VMEM((8, TILE), i32),
            pltpu.VMEM((16, 8, TILE), i32),
            pltpu.SMEM((16, 8, TILE), i32),
            pltpu.VMEM((2 * TILE, A_ROWS), bf16),
            pltpu.VMEM((2, A_ROWS, 2 * TILE), bf16),
            pltpu.VMEM((16, 2, TILE, TILE), f32),
            dma((6,)),
            dma((16,)),
            dma((17,)),
            dma((16,)),
            dma((N_ROW,)),
            dma((N_ROW,)),
            dma((17,)),
            dma((18,)),
            dma((25,)),
            dma((25,)),
            dma((16, 2)),
            dma((16, 2)),
            pltpu.SemaphoreType.REGULAR,
        ],
        compiler_params=pltpu.CompilerParams(
            collective_id=0, has_side_effects=True, vmem_limit_bytes=48 * 2**20
        ),
        cost_estimate=pl.CostEstimate(
            flops=6 * 16 * 28 * TILE**3, bytes_accessed=4 * 2**20, transcendentals=0
        ),
        name="gather_multiply_sum",
    )(
        hbm(c_cols.reshape(16, 4).T),
        hbm(a_cols),
        hbm(b_rows),
        hbm(a_tiles.reshape(A_ROWS, TILE)),
        hbm(b_tiles.reshape(B_ROWS, TILE)),
    )
    out = pl.pallas_call(
        add_kernel,
        out_shape=part,
        in_specs=[in_vmem, in_vmem],
        out_specs=in_hbm,
        scratch_shapes=[pltpu.VMEM((16, 2, TILE, TILE), f32), dma((4,))],
        compiler_params=pltpu.CompilerParams(vmem_limit_bytes=8 * 2**20),
        name="add_halves",
    )(own, arrived)
    return out[:, None]


def solution(mesh):
    return jax.shard_map(
        on_device,
        mesh=mesh,
        in_specs=(
            P(("row", "col"), "layer", None, None, None),
            P(("row", "col"), "layer", None),
            P(("row", "col"), "layer", None, None, None),
            P(("row", "col"), "layer", None),
            P("row", "col", None),
        ),
        out_specs=P("row", "col", "layer", None, None),
        check_vma=False,
    )
```
